32 devices in a mesh: seq: 8 (over z, x), tp: 4 (over y, core).
Axes of the slice: x: 2, y: 2, z: 4, core: 2. Of those that a mesh axis runs over, the one named last changes fastest.
Arguments:
- hidden_new: bfloat16 [3, 16, 8192], P(None, None, 'seq'), may hold values from -6 to 6
- w_kv: bfloat16 [8192, 8, 256], P('seq', 'tp'), may hold values from -0.0625 to 0.0625
- w_out: bfloat16 [8192, 8192], P('tp', 'seq'), may hold values from -0.0625 to 0.0625
- queries_draft: bfloat16 [3, 4, 8, 32, 128], P(None, None, 'tp'), may hold values from -48 to 48
- queries_verify: bfloat16 [3, 4, 8, 32, 128], P(None, None, 'tp'), may hold values from -48 to 48
- keys_cache: bfloat16 [4, 8, 16384, 128], P(None, 'tp', 'seq'), may hold values from -6 to 6
- values_cache: bfloat16 [4, 8, 16384, 128], P(None, 'tp', 'seq'), may hold values from -6 to 6
- key_levels: bfloat16 [4, 8, 16384, 128], P(None, 'tp', 'seq'), may hold values from -8 to 7, as said below
- value_levels: bfloat16 [4, 8, 16384, 128], P(None, 'tp', 'seq'), may hold values from -8 to 7, as said below
- key_scales: float32 [4, 8, 16384], P(None, 'tp', 'seq'), may hold values from 0.05 to 0.5
- value_scales: float32 [4, 8, 16384], P(None, 'tp', 'seq'), may hold values from 0.1 to 0.4
- lengths: int32 [4], replicated, may hold values from 2 to 16376, as said below
- accepted: int32 [2, 4], replicated, may hold values from 0 to 4, as said below
Outputs:
- layer_out: bfloat16 [3, 2, 16, 8192], P(None, None, None, 'seq')
The draws below stay inside these ranges and needn't reach their ends.
Inputs may be any that keep to these rules, and one draw needn't show every extreme that they name: `key_levels`: every entry is a whole number. Positions 0 and 1 of every sequence and head hold equal levels. `value_levels`: every entry is a whole number. `lengths`: some sequence starts with exactly 16376 valid positions, another with 16 or fewer. `accepted`: the values 0 and 4 both occur.
All inputs are finite; a program needn't handle non-finite values.
Results may differ from the reference program's by a relative error of at most 0.006.
The reference program's roundings to bfloat16 on the way count: a program that leaves them out, or rounds other values in their place, can miss the bound.
Values may be sent and summed in bfloat16 or wider, within the bound.
A program may use at most 128 MiB of HBM per device.

```python
import math
import jax
import jax.numpy as jnp
from jax import lax

D = 8192
KVH = 8
HD = 128
GROUP = 8
B = 4
S_DEV = 2048
R = 4
ROUNDS = 3
CTX = 16384
N_SEQ = 8


def first_levels(key):
    return jax.random.randint(jax.random.fold_in(key, 902), (B, KVH, HD), -8, 8, dtype=jnp.int32).astype(jnp.float32)


def broad_rows(key, label, base_rows):
    shape_full = (ROUNDS, B, KVH, GROUP * R, HD)
    chosen = jax.random.randint(jax.random.fold_in(key, label), (ROUNDS, B, KVH, GROUP * R), 0, 8) == 0
    signs = jnp.where(jax.random.bernoulli(jax.random.fold_in(key, label + 1), 0.5, shape_full), 1.0, -1.0)
    magnitude = jax.random.uniform(jax.random.fold_in(key, label + 2), shape_full, jnp.float32, 24.0, 48.0)
    return jnp.where(chosen[..., None], signs * magnitude, base_rows)


def draw_queries_draft(key, part):
    base_rows = jnp.clip(3.0 * jax.random.normal(jax.random.fold_in(key, 31), (ROUNDS, B, KVH, GROUP * R, HD), jnp.float32), -12.0, 12.0)
    base_rows = broad_rows(key, 71, base_rows)
    return base_rows.astype(jnp.bfloat16)


def draw_queries_verify(key, part):
    base_rows = jnp.clip(3.0 * jax.random.normal(jax.random.fold_in(key, 32), (ROUNDS, B, KVH, GROUP * R, HD), jnp.float32), -12.0, 12.0)
    base_rows = broad_rows(key, 81, base_rows)
    return base_rows.astype(jnp.bfloat16)


def draw_keys_cache(key, part):
    base_rows = jnp.clip(jax.random.normal(jax.random.fold_in(key, 33), (B, KVH, CTX, HD), jnp.float32), -6.0, 6.0)
    return base_rows.astype(jnp.bfloat16)


def draw_key_scales(key, part):
    uniform_log = jax.random.uniform(jax.random.fold_in(key, 34), (B, KVH, CTX), jnp.float32)
    scales = jnp.exp(math.log(0.15) + uniform_log * (math.log(0.3) - math.log(0.15)))
    return scales


def draw_key_levels(key, part):
    levels = jax.random.randint(jax.random.fold_in(key, 61), (B, KVH, CTX, HD), -8, 8, dtype=jnp.int32).astype(jnp.float32)
    leading = first_levels(key)
    levels = levels.at[:, :, 0, :].set(leading).at[:, :, 1, :].set(leading)
    return levels.astype(jnp.bfloat16)


def draw_value_levels(key, part):
    levels = jax.random.randint(jax.random.fold_in(key, 62), (B, KVH, CTX, HD), -8, 8, dtype=jnp.int32).astype(jnp.float32)
    return levels.astype(jnp.bfloat16)


def draw_lengths(key, part):
    longest = CTX - (ROUNDS - 1) * R
    top_bits = max(longest.bit_length() - 1, 1)
    exponents = jax.random.randint(jax.random.fold_in(key, 51), (B,), 1, top_bits + 1, dtype=jnp.int32)
    lowest = jnp.left_shift(jnp.ones((B,), jnp.int32), exponents)
    values_drawn = jax.random.randint(jax.random.fold_in(key, 52), (B,), lowest, 2 * lowest, dtype=jnp.int32)
    values_drawn = jnp.clip(values_drawn, 2, longest)
    picked = jax.random.randint(jax.random.fold_in(key, 55), (), 0, B, dtype=jnp.int32)
    other = (picked + jax.random.randint(jax.random.fold_in(key, 56), (), 1, B, dtype=jnp.int32)) % B
    short_len = jax.random.randint(jax.random.fold_in(key, 57), (), 2, min(17, longest + 1), dtype=jnp.int32)
    return values_drawn.at[picked].set(longest).at[other].set(short_len).astype(jnp.int32)


def draw_accepted(key, part):
    counts = jax.random.randint(jax.random.fold_in(key, 53), ((ROUNDS - 1) * B,), 0, R + 1, dtype=jnp.int32)
    picked = jax.random.permutation(jax.random.fold_in(key, 54), (ROUNDS - 1) * B)
    counts = counts.at[picked[0]].set(R).at[picked[1]].set(0)
    return counts.reshape(ROUNDS - 1, B).astype(jnp.int32)


def block_scale(rng, shape, pieces, least, top_value):
    loudness = 1.0
    for dim, blocks in pieces:
        steps = jax.random.uniform(jax.random.fold_in(jax.random.fold_in(rng, 6), dim), (blocks,), jnp.float32, least / len(pieces), top_value / len(pieces))
        loudness = loudness * jnp.repeat(jnp.exp(steps), shape[dim] // blocks).reshape((-1,) + (1,) * (len(shape) - 1 - dim))
    return loudness


def scatter_about(stream_key, shape, width, limit, split=(), held_as=jnp.bfloat16):
    result = jax.random.normal(stream_key, shape, jnp.float32) * width
    if len(split) > 0:
        result = block_scale(stream_key, shape, split, -0.22, 0.18) * result
    return jnp.clip(result, min=-limit, max=limit).astype(held_as)


def setup_inputs(seed: int = 0) -> dict:
    arg_keys = jax.random.split(jax.random.key(seed), 14)
    return {
        "hidden_new": scatter_about(arg_keys[0], (ROUNDS, B * R, D), 1.0, 6.0, ((2, 8),)),
        "w_kv": scatter_about(arg_keys[1], (D, KVH, 2 * HD), D ** -0.5, 0.0625, ((0, 8), (1, 4))),
        "w_out": scatter_about(arg_keys[2], (KVH * GROUP * HD, D), (KVH * GROUP * HD) ** -0.5, 0.0625, ((0, 4), (1, 8))),
        "queries_draft": draw_queries_draft(jax.random.fold_in(arg_keys[13], 71), 0),
        "queries_verify": draw_queries_verify(jax.random.fold_in(arg_keys[13], 71), 0),
        "keys_cache": draw_keys_cache(jax.random.fold_in(arg_keys[13], 71), 0),
        "values_cache": scatter_about(arg_keys[6], (B, KVH, CTX, HD), 1.0, 6.0, ((1, 4), (2, 8))),
        "key_levels": draw_key_levels(jax.random.fold_in(arg_keys[13], 71), 0),
        "value_levels": draw_value_levels(jax.random.fold_in(arg_keys[13], 71), 0),
        "key_scales": draw_key_scales(jax.random.fold_in(arg_keys[13], 71), 0),
        "value_scales": jnp.clip(jnp.exp(math.log(0.4) - 1.3862944 * jax.random.uniform(arg_keys[10], (B, KVH, CTX), jnp.float32) ** block_scale(arg_keys[10], (B, KVH, CTX), ((1, 4), (2, 8)), -0.2, 0.2)), 0.1, 0.4),
        "lengths": draw_lengths(jax.random.fold_in(arg_keys[13], 71), 0),
        "accepted": draw_accepted(jax.random.fold_in(arg_keys[13], 71), 0),
    }


NEG = -1e+30

def dequantize(levels, scales):
    return (levels.astype(jnp.float32) * scales[..., None]).astype(jnp.bfloat16)

def attend(queries, keys, values, usable):
    scores = jnp.einsum('bhqd,bhkd->bhqk', queries.astype(jnp.float32), keys.astype(jnp.float32)) * (1.0 / math.sqrt(HD))
    scores = jnp.where(usable, scores, NEG)
    maxima = lax.optimization_barrier(jnp.max(scores, axis=-1))
    weights = jnp.where(usable, jnp.exp(scores - maxima[..., None]), 0.0).astype(jnp.bfloat16)
    totals = lax.optimization_barrier(jnp.sum(weights.astype(jnp.float32), axis=-1))
    weighted = jnp.einsum('bhqk,bhkd->bhqd', weights.astype(jnp.float32), values.astype(jnp.float32))
    return (maxima, totals, weighted)

def combine(former, latter):
    highest = jnp.maximum(former[0], latter[0])
    former_w = jnp.exp(former[0] - highest)
    latter_w = jnp.exp(latter[0] - highest)
    return (highest, former[1] * former_w + latter[1] * latter_w, former[2] * former_w[..., None] + latter[2] * latter_w[..., None])

def finish(partial_value):
    return (partial_value[2] / partial_value[1][..., None]).astype(jnp.bfloat16)

def arrange(attended):
    return attended.reshape(2, B, KVH, GROUP, R, HD).transpose(0, 1, 4, 2, 3, 5).reshape(2 * B * R, KVH * GROUP * HD)

def reference(hidden_new, w_kv, w_out, queries_draft, queries_verify, keys_cache, values_cache, key_levels, value_levels, key_scales, value_scales, lengths, accepted):
    flat_kv = w_kv.reshape(D, KVH * 2 * HD)
    tokens = jnp.arange(GROUP * R, dtype=jnp.int32) % R
    causal = (tokens[:, None] >= jnp.arange(R, dtype=jnp.int32)[None, :])[None, None]
    offsets = jnp.arange(R, dtype=jnp.int32)[None, :]
    batch_rows = jnp.broadcast_to(jnp.arange(B, dtype=jnp.int32)[:, None], (B, R))
    blocks = jnp.arange(N_SEQ, dtype=jnp.int32)
    length_now = lengths
    results = []
    for turn_index in range(ROUNDS):
        fresh_rows = jnp.dot(hidden_new[turn_index], flat_kv, preferred_element_type=jnp.float32).astype(jnp.bfloat16).reshape(B, R, KVH, 2, HD)
        new_keys = fresh_rows[:, :, :, 0].transpose(0, 2, 1, 3)
        new_values = fresh_rows[:, :, :, 1].transpose(0, 2, 1, 3)
        draft_q = queries_draft[turn_index]
        verify_q = queries_verify[turn_index]

        def visit(running, block_index):
            first_row = block_index * S_DEV
            key_rows = lax.dynamic_slice_in_dim(keys_cache, first_row, S_DEV, 2)
            value_rows = lax.dynamic_slice_in_dim(values_cache, first_row, S_DEV, 2)
            key_low = dequantize(lax.dynamic_slice_in_dim(key_levels, first_row, S_DEV, 2), lax.dynamic_slice_in_dim(key_scales, first_row, S_DEV, 2))
            value_low = dequantize(lax.dynamic_slice_in_dim(value_levels, first_row, S_DEV, 2), lax.dynamic_slice_in_dim(value_scales, first_row, S_DEV, 2))
            places = first_row + jnp.arange(S_DEV, dtype=jnp.int32)
            stored = (places[None, :] < lengths[:, None])[:, None, :, None]
            usable = (places[None, :] < length_now[:, None])[:, None, None, :]
            draft_keys = jnp.where(stored, key_low, key_rows)
            draft_values = jnp.where(stored, value_low, value_rows)
            draft_part = attend(draft_q, draft_keys, draft_values, usable)
            verify_part = attend(verify_q, key_rows, value_rows, usable)
            return ((combine(running[0], draft_part), combine(running[1], verify_part)), None)
        initial = (jnp.full((B, KVH, GROUP * R), NEG, jnp.float32), jnp.zeros((B, KVH, GROUP * R), jnp.float32), jnp.zeros((B, KVH, GROUP * R, HD), jnp.float32))
        merged, unused = lax.scan(visit, (initial, initial), blocks)
        draft_all = combine(merged[0], attend(draft_q, new_keys, new_values, causal))
        verify_all = combine(merged[1], attend(verify_q, new_keys, new_values, causal))
        attended = jnp.stack([finish(draft_all), finish(verify_all)])
        projected = jnp.dot(arrange(attended), w_out, preferred_element_type=jnp.float32)
        results.append(projected.astype(jnp.bfloat16).reshape(2, B * R, D))
        if turn_index + 1 < ROUNDS:
            accepted_now = accepted[turn_index]
            places = jnp.where(offsets < accepted_now[:, None], length_now[:, None] + offsets, CTX)
            keys_cache = keys_cache.at[batch_rows, :, places, :].set(fresh_rows[:, :, :, 0], mode='drop')
            values_cache = values_cache.at[batch_rows, :, places, :].set(fresh_rows[:, :, :, 1], mode='drop')
            length_now = length_now + accepted_now
    return jnp.stack(results)
```

```python
import functools
import math

import jax
import jax.numpy as jnp
from jax import lax
from jax.experimental import pallas as pl
from jax.experimental.pallas import tpu as pltpu
from jax.sharding import PartitionSpec as P

NEG = -1e30
LANES = 128
F32 = jnp.float32
BF16 = jnp.bfloat16
MESH = pl.DeviceIdType.MESH


def onehot(rows, cols, source):
    r = lax.broadcasted_iota(jnp.int32, (rows, cols), 0)
    c = lax.broadcasted_iota(jnp.int32, (rows, cols), 1)
    return (source(r) == c).astype(F32).astype(BF16)


def kernel(cfg, *refs):
    (len_s, acc_s, hid_h, ks_h, vs_h, qd_h, qv_h, wkv_h, wout_h, k_h, v_h, kl_h, vl_h, out_ref,
     hid_v, ks_v, vs_v, qd_v, qv_v, wkv, wout, kc, vc, kl, vl, sc_a, sc_b, m_a, m_b, sel,
     fr_send, fr_recv, o_send, o_recv, st_send, st_recv, ag,
     rs_send, rs_recv, y_buf, fin_send, fin_recv,
     in_sem, kv_sem, frs_sem, frr_sem, os_sem, or_sem, ss_sem, sr_sem,
     ags_sem, agf_sem, agr_sem, rss_sem, rsr_sem, ys_sem, yr_sem, fs_sem, ffr_sem) = refs
    n, tp, batch, heads, rounds, R, group, S, HD, CH = cfg
    pairs = batch * heads
    k = n // pairs
    rows1 = rounds * group * R
    fpad = fr_send.shape[1]
    feats = hid_v.shape[1]
    ys = tp // 2
    me = lax.axis_index("seq")
    tpi = lax.axis_index("tp")
    mine = lax.div(me, k)
    sub = lax.rem(me, k)
    core = lax.rem(tpi, 2)
    sib = tpi + 1 - 2 * core
    yi = lax.div(tpi, 2)
    DRAFT, VERIFY = 0, 1

    split_w = heads > 1
    if split_w:
        cp_wkv = [
            pltpu.make_async_copy(wkv_h.at[:, :, c * LANES:(c + 1) * LANES], wkv.at[c], in_sem.at[c])
            for c in range(2 * HD // LANES)
        ]
    else:
        cp_wkv = [pltpu.make_async_copy(wkv_h, wkv, in_sem.at[0])]
    base = 2 * HD // LANES
    cp_hid, cp_ks, cp_vs, cp_qd, cp_qv, cp_wout = [
        pltpu.make_async_copy(s, d, in_sem.at[base + j])
        for j, (s, d) in enumerate(((hid_h, hid_v), (ks_h, ks_v), (vs_h, vs_v), (qd_h, qd_v), (qv_h, qv_v),
                                    (wout_h, wout)))
    ]

    def place_of(u):
        return lax.rem(mine + 1 + u, pairs)

    def cache_copies(kind, p):
        b = lax.div(p, heads)
        h = lax.rem(p, heads)
        arrays = ((kl_h, kl), (vl_h, vl)) if kind == DRAFT else ((k_h, kc), (v_h, vc))
        return [
            pltpu.make_async_copy(src.at[b, h], dst.at[p], kv_sem.at[2 * kind + j, p])
            for j, (src, dst) in enumerate(arrays)
        ]

    cp_hid.start()
    for c in cp_wkv:
        c.start()
    cp_qd.start()
    cp_ks.start()
    cp_vs.start()
    for kind in (DRAFT, VERIFY):
        for u in range(pairs):
            for c in cache_copies(kind, place_of(u)):
                c.start()
        if kind == DRAFT:
            cp_qv.start()
    cp_wout.start()

    barrier = pltpu.get_barrier_semaphore()
    for j in range(1, n):
        pl.semaphore_signal(barrier, inc=1, device_id={"seq": lax.rem(me + j, n)}, device_id_type=MESH)
    pl.semaphore_signal(barrier, inc=1, device_id={"tp": sib}, device_id_type=MESH)
    y_peers = [lax.rem(yi + j, ys) for j in range(1, ys)]
    for y in y_peers:
        pl.semaphore_signal(barrier, inc=1, device_id={"tp": 2 * y + core}, device_id_type=MESH)

    tok = rounds * batch * R

    def fresh_source(r):
        b, q = r // fpad, r % fpad
        return jnp.where(q < rounds * R, (q // R) * (batch * R) + b * R + q % R, tok)

    frows = batch * fpad
    cp_hid.wait()
    hid = jnp.dot(onehot(frows, tok, fresh_source), hid_v[...], preferred_element_type=F32).astype(BF16)
    if split_w:
        blocks = feats // LANES
        stack = jnp.concatenate([hid[:, j * LANES:(j + 1) * LANES] for j in range(blocks)], axis=0)
        lhs = []
        for h in range(heads):
            r = lax.broadcasted_iota(jnp.int32, (LANES, heads * LANES), 0)
            c = lax.broadcasted_iota(jnp.int32, (LANES, heads * LANES), 1)
            spread = (heads * r + h == c).astype(F32).astype(BF16)
            wide = jnp.dot(stack, spread, preferred_element_type=F32).astype(BF16)
            lhs.append(jnp.concatenate([wide[j * frows:(j + 1) * frows] for j in range(blocks)], axis=1))
        lhs = jnp.concatenate(lhs, axis=0)
        for c, cp in enumerate(cp_wkv):
            cp.wait()
            part = jnp.dot(lhs, wkv[c].reshape(feats * heads, LANES), preferred_element_type=F32)
            for p in range(pairs):
                b, h = p // heads, p % heads
                fr_send[p, :, c * LANES:(c + 1) * LANES] = part[h * frows + b * fpad:h * frows + (b + 1) * fpad]
    else:
        cp_wkv[0].wait()
        part = jnp.dot(hid, wkv[:, 0, :], preferred_element_type=F32)
        for b in range(batch):
            fr_send[b] = part[b * fpad:(b + 1) * fpad]

    def fresh_copy(dst, slot):
        return pltpu.make_async_remote_copy(
            src_ref=fr_send.at[lax.div(dst, k)], dst_ref=fr_recv.at[slot],
            send_sem=frs_sem.at[dst], recv_sem=frr_sem.at[slot],
            device_id={"seq": dst}, device_id_type=MESH)

    fr_recv[me] = fr_send[mine]

    toks = rounds * batch * R

    def sel_source(r):
        g, q = r // toks, r % toks
        t, q = q // (batch * R), q % (batch * R)
        return (q // R) * rows1 + t * (group * R) + g * R + q % R

    sel[...] = onehot(group * toks, batch * rows1, sel_source)

    factor = (1.0 / math.sqrt(HD)) * math.log2(math.e)
    eye = (lax.broadcasted_iota(jnp.int32, (LANES, LANES), 0)
           == lax.broadcasted_iota(jnp.int32, (LANES, LANES), 1))[:rows1]

    def to_row(full):
        return jnp.sum(jnp.where(eye, full, 0.0), axis=0, keepdims=True)

    per = CH // LANES
    chunks = S // CH

    def scale_columns(r, b, h):
        row = jnp.where(h == 0, r[b, 0:1, :], r[b, heads - 1:heads, :])
        cut = [row[:, c * LANES:(c + 1) * LANES] for c in range(S // LANES)]
        cut += [cut[0]] * (-len(cut) % 8)
        return jnp.concatenate(cut, axis=0).T

    def low(levels, p, scales, c):
        parts = []
        for j in range(c * per, (c + 1) * per):
            parts.append((levels[p, j * LANES:(j + 1) * LANES].astype(F32) * scales[:, j:j + 1]).astype(BF16))
        return jnp.concatenate(parts, axis=0)

    def score(kind, u, sc, m_ref):
        p = place_of(u)
        b, h = lax.div(p, heads), lax.rem(p, heads)
        count = len_s[b] - me * S
        q = (qd_v if kind == DRAFT else qv_v)[:, b, h].reshape(rows1, HD)
        if kind == DRAFT:
            scales = scale_columns(ks_v, b, h)
        top = None
        for c in range(chunks):
            keys = low(kl, p, scales, c) if kind == DRAFT else kc[p, c * CH:(c + 1) * CH]
            s = lax.dot_general(q, keys, (((1,), (1,)), ((), ())), preferred_element_type=F32)
            s = jnp.where(lax.broadcasted_iota(jnp.int32, (1, CH), 1) + c * CH < count, s, NEG)
            sc[:, c * CH:(c + 1) * CH] = s
            for j in range(per):
                piece = s[:, j * LANES:(j + 1) * LANES]
                top = piece if top is None else jnp.maximum(top, piece)
        m = jnp.max(top, axis=1, keepdims=True) * factor
        m_ref[...] = jnp.broadcast_to(m, (rows1, LANES))

    def weigh(kind, u, sc, m_ref, o_dst, st_dst):
        p = place_of(u)
        b, h = lax.div(p, heads), lax.rem(p, heads)
        count = len_s[b] - me * S
        if kind == DRAFT:
            scales = scale_columns(vs_v, b, h)
        m = m_ref[...]
        acc = None
        for c in range(chunks):
            w = jnp.concatenate(
                [jnp.exp2(sc[:, j * LANES:(j + 1) * LANES] * factor - m).astype(BF16)
                 for j in range(c * per, (c + 1) * per)], axis=1)
            values = low(vl, p, scales, c) if kind == DRAFT else vc[p, c * CH:(c + 1) * CH]
            both = jnp.dot(w, jnp.concatenate([values, jnp.ones((CH, LANES), BF16)], axis=1),
                           preferred_element_type=F32)
            acc = both if acc is None else acc + both
        l = acc[:, HD:]
        o_dst[...] = (acc[:, :HD] / l).astype(BF16)
        lse = to_row(m + jnp.log2(l))
        st_dst[...] = jnp.where(jnp.full(lse.shape, count) > 0, lse, NEG)

    def o_copy(kind, p, dst, slot, src):
        return pltpu.make_async_remote_copy(
            src_ref=src, dst_ref=o_recv.at[kind, slot], send_sem=os_sem.at[kind, dst],
            recv_sem=or_sem.at[kind, slot], device_id={"seq": dst}, device_id_type=MESH)

    def s_copy(kind, p, dst, slot, src):
        return pltpu.make_async_remote_copy(
            src_ref=src, dst_ref=st_recv.at[kind, slot], send_sem=ss_sem.at[kind, dst],
            recv_sem=sr_sem.at[kind, slot], device_id={"seq": dst}, device_id_type=MESH)

    def send_pair(kind, u):
        p = place_of(u)
        for e in range(k):
            dst = p * k + lax.rem(sub + e, k)
            o_copy(kind, p, dst, me, o_send.at[kind, p]).start()
            s_copy(kind, p, dst, me, st_send.at[kind, p]).start()

    def send_mine(kind):
        for e in range(1, k):
            dst = mine * k + lax.rem(sub + e, k)
            o_copy(kind, mine, dst, me, o_recv.at[kind, me]).start()
            s_copy(kind, mine, dst, me, st_recv.at[kind, me]).start()

    def arrived(kind, u):
        for c in cache_copies(kind, place_of(u)):
            c.wait()

    def both_to(kind, u):
        p = place_of(u)
        return o_send.at[kind, p], st_send.at[kind, p]

    bm = lax.div(mine, heads)
    hm = lax.rem(mine, heads)

    def fresh_part(kind):
        total = fr_recv[0]
        for j in range(1, n):
            total = total + fr_recv[j]
        new_k = total[:, :HD].astype(BF16)
        new_v = total[:, HD:].astype(BF16)
        r_id = lax.broadcasted_iota(jnp.int32, (rows1, fpad), 0)
        c_id = lax.broadcasted_iota(jnp.int32, (rows1, fpad), 1)
        turn, i_q = r_id // (group * R), r_id % R
        c_turn, c_j = c_id // R, c_id % R
        limit = jnp.zeros((rows1, fpad), jnp.int32)
        for t in range(rounds - 1):
            limit = jnp.where(c_turn == t, acc_s[t, bm], limit)
        see = ((c_turn < turn) & (c_j < limit)) | ((c_turn == turn) & (c_j <= i_q))
        q = (qd_v if kind == DRAFT else qv_v)[:, bm, hm].reshape(rows1, HD)
        s = lax.dot_general(q, new_k, (((1,), (1,)), ((), ())), preferred_element_type=F32)
        s = jnp.where(see, s, NEG)
        m = jnp.max(s, axis=1, keepdims=True) * factor
        w = jnp.exp2(s * factor - m).astype(BF16)
        both = jnp.dot(w, jnp.concatenate([new_v, jnp.ones(new_v.shape, BF16)], axis=1), preferred_element_type=F32)
        l = both[:, HD:]
        return to_row(m + jnp.log2(l)), both[:, :HD] / l

    def combine(kind):
        row, o_new = fresh_part(kind)
        for j in range(1, n):
            src = lax.rem(me + j, n)
            o_copy(kind, mine, src, src, o_send.at[kind, 0]).wait_recv()
            s_copy(kind, mine, src, src, st_send.at[kind, 0]).wait_recv()
        lse = jnp.concatenate([row] + [st_recv[kind, j] for j in range(n)] + [jnp.full(row.shape, NEG)] * (-(n + 1) % 8),
                              axis=0)
        w = jnp.exp2(lse - jnp.max(lse, axis=0, keepdims=True))
        w = (w / jnp.sum(w, axis=0, keepdims=True)).T
        total = o_new * w[:rows1, 0:1]
        for j in range(n):
            total = total + o_recv[kind, j].astype(F32) * w[:rows1, j + 1:j + 2]
        ag[kind, mine] = total.astype(BF16)

    partner = mine + 1 - 2 * lax.rem(mine, 2)
    others = [lax.rem(mine + 2 * j, pairs) for j in range(1, pairs // 2)]
    across = [lax.rem(partner + 2 * j, pairs) for j in range(1, pairs // 2)]
    order = sorted(range(len(others)), key=lambda j: abs(j + 1 - pairs / 4))

    def ag_copy(kind, slot, to, sem):
        return pltpu.make_async_remote_copy(
            src_ref=ag.at[kind, slot], dst_ref=ag.at[kind, slot], send_sem=sem, recv_sem=agr_sem.at[kind, slot],
            device_id={"seq": to * k + sub}, device_id_type=MESH)

    def spread_rows(kind, direct):
        for j in order:
            ag_copy(kind, mine, others[j], ags_sem.at[kind, others[j]]).start()
        ag_copy(kind, mine, partner, ags_sem.at[kind, partner]).start()
        if direct:
            for q in across:
                ag_copy(kind, mine, q, ags_sem.at[kind, q]).start()

    far = [others[j] for j in reversed(order)]

    def forward_rows(kind):
        for q in far:
            ag_copy(kind, q, partner, agf_sem.at[q]).wait_recv()
            ag_copy(kind, q, partner, agf_sem.at[q]).start()

    def gathered(kind, direct):
        for q in ([partner] + across) + (others if direct else []):
            ag_copy(kind, q, partner, agf_sem.at[q]).wait_recv()

    last = pairs - 1
    hold = min(1, pairs // 2 - 2)

    cp_qd.wait()
    cp_ks.wait()
    cp_vs.wait()
    arrived(DRAFT, 0)
    score(DRAFT, 0, sc_a, m_a)

    @pl.loop(0, pairs // 2 - 1)
    def _(i):
        u = 2 * i
        arrived(DRAFT, u + 1)
        score(DRAFT, u + 1, sc_b, m_b)
        weigh(DRAFT, u, sc_a, m_a, *both_to(DRAFT, u))
        arrived(DRAFT, u + 2)
        score(DRAFT, u + 2, sc_a, m_a)
        weigh(DRAFT, u + 1, sc_b, m_b, *both_to(DRAFT, u + 1))

        @pl.when(i == hold)
        def _():
            pl.semaphore_wait(barrier, n - 1 + ys)
            for j in range(1, n):
                fresh_copy(lax.rem(me + j, n), me).start()
            for v in range(2 * hold):
                send_pair(DRAFT, v)

        @pl.when(i >= hold)
        def _():
            send_pair(DRAFT, u)
            send_pair(DRAFT, u + 1)

    arrived(DRAFT, last)
    score(DRAFT, last, sc_b, m_b)
    weigh(DRAFT, last - 1, sc_a, m_a, *both_to(DRAFT, last - 1))
    send_pair(DRAFT, last - 1)
    cp_qv.wait()
    arrived(VERIFY, 0)
    score(VERIFY, 0, sc_a, m_a)
    weigh(DRAFT, last, sc_b, m_b, o_recv.at[DRAFT, me], st_recv.at[DRAFT, me])
    send_mine(DRAFT)

    @pl.loop(0, pairs // 2 - 1)
    def _(i):
        u = 2 * i
        arrived(VERIFY, u + 1)
        score(VERIFY, u + 1, sc_b, m_b)
        weigh(VERIFY, u, sc_a, m_a, *both_to(VERIFY, u))
        send_pair(VERIFY, u)
        arrived(VERIFY, u + 2)
        score(VERIFY, u + 2, sc_a, m_a)
        weigh(VERIFY, u + 1, sc_b, m_b, *both_to(VERIFY, u + 1))
        send_pair(VERIFY, u + 1)

        @pl.when(i == hold)
        def _():
            for j in range(1, n):
                fresh_copy(lax.rem(me + j, n), lax.rem(me + j, n)).wait_recv()
            combine(DRAFT)
            spread_rows(DRAFT, False)

    arrived(VERIFY, last)
    score(VERIFY, last, sc_b, m_b)
    weigh(VERIFY, last - 1, sc_a, m_a, *both_to(VERIFY, last - 1))
    send_pair(VERIFY, last - 1)
    weigh(VERIFY, last, sc_b, m_b, o_recv.at[VERIFY, me], st_recv.at[VERIFY, me])
    send_mine(VERIFY)

    forward_rows(DRAFT)
    combine(VERIFY)
    spread_rows(VERIFY, True)

    depth = group * HD
    half = rs_send.shape[2]

    def lhs_of(kind):
        out = []
        for h in range(heads):
            rows = jnp.concatenate([ag[kind, b * heads + h] for b in range(batch)], axis=0)
            y = jnp.dot(sel[...], rows, preferred_element_type=F32)
            out.append(jnp.concatenate([y[g * toks:(g + 1) * toks] for g in range(group)], axis=1).astype(BF16))
        return out

    def columns(c):
        return pl.ds(pl.multiple_of(c * half, LANES), half)

    def project(lhs, c):
        acc = jnp.dot(lhs[0], wout[0:depth, columns(c)], preferred_element_type=F32)
        for h in range(1, heads):
            acc += jnp.dot(lhs[h], wout[h * depth:(h + 1) * depth, columns(c)], preferred_element_type=F32)
        return acc

    def rs_copy(kind):
        return pltpu.make_async_remote_copy(
            src_ref=rs_send.at[kind], dst_ref=rs_recv.at[kind], send_sem=rss_sem.at[kind],
            recv_sem=rsr_sem.at[kind], device_id={"tp": sib}, device_id_type=MESH)

    def y_copy(kind, slot, to):
        return pltpu.make_async_remote_copy(
            src_ref=y_buf.at[kind, slot], dst_ref=y_buf.at[kind, slot], send_sem=ys_sem.at[kind, to],
            recv_sem=yr_sem.at[kind, slot], device_id={"tp": 2 * to + core}, device_id_type=MESH)

    def fin_copy(kind):
        return pltpu.make_async_remote_copy(
            src_ref=fin_send.at[kind], dst_ref=fin_recv.at[kind], send_sem=fs_sem.at[kind],
            recv_sem=ffr_sem.at[kind], device_id={"tp": sib}, device_id_type=MESH)

    def first_sum(kind):
        lhs = lhs_of(kind)
        rs_send[kind] = project(lhs, 1 - core).astype(BF16)
        rs_copy(kind).start()
        return project(lhs, core)

    def second_sum(kind, own):
        rs_copy(kind).wait_recv()
        y_buf[kind, yi] = (own + rs_recv[kind].astype(F32)).astype(BF16)
        for y in y_peers:
            y_copy(kind, yi, y).start()

    def put(kind, c, value):
        out_ref[:, kind, :, columns(c)] = value.reshape(rounds, batch * R, half)

    def third_sum(kind):
        for y in y_peers:
            y_copy(kind, y, y).wait_recv()
        total = y_buf[kind, 0].astype(F32)
        for y in range(1, ys):
            total = total + y_buf[kind, y].astype(F32)
        total = total.astype(BF16)
        fin_send[kind] = total
        fin_copy(kind).start()
        put(kind, core, total)

    def finish(kind):
        fin_copy(kind).wait_recv()
        put(kind, 1 - core, fin_recv[kind])

    cp_wout.wait()
    gathered(DRAFT, False)
    own_d = first_sum(DRAFT)
    second_sum(DRAFT, own_d)
    gathered(VERIFY, True)
    own_v = first_sum(VERIFY)
    third_sum(DRAFT)
    second_sum(VERIFY, own_v)
    finish(DRAFT)
    third_sum(VERIFY)
    finish(VERIFY)

    for j in range(1, n):
        dst = lax.rem(me + j, n)
        fresh_copy(dst, me).wait_send()
        for kind in (DRAFT, VERIFY):
            o_copy(kind, 0, dst, me, o_send.at[kind, 0]).wait_send()
            s_copy(kind, 0, dst, me, st_send.at[kind, 0]).wait_send()
    for kind in (DRAFT, VERIFY):
        for q in others + [partner] + (across if kind == VERIFY else []):
            ag_copy(kind, mine, q, ags_sem.at[kind, q]).wait_send()
        rs_copy(kind).wait_send()
        fin_copy(kind).wait_send()
        for y in y_peers:
            y_copy(kind, yi, y).wait_send()
    for q in far:
        ag_copy(DRAFT, q, partner, agf_sem.at[q]).wait_send()


def per_device(n, tp, hidden_new, w_kv, w_out, queries_draft, queries_verify, keys_cache,
               values_cache, key_levels, value_levels, key_scales, value_scales, lengths, accepted):
    batch, heads, S, HD = keys_cache.shape
    rounds = hidden_new.shape[0]
    R = hidden_new.shape[1] // batch
    group = queries_draft.shape[3] // R
    pairs = batch * heads
    feats = hidden_new.shape[2]
    cols = w_out.shape[1]
    rows1 = rounds * group * R
    toks = rounds * batch * R
    fpad = -(-rounds * R // 16) * 16
    half = cols // 2
    ys = tp // 2
    chunk = 2 * LANES
    cfg = (n, tp, batch, heads, rounds, R, group, S, HD, chunk)
    sm = pl.BlockSpec(memory_space=pltpu.SMEM)
    hb = pl.BlockSpec(memory_space=pltpu.HBM)
    dma = lambda *shape: pltpu.SemaphoreType.DMA(shape)
    vb = lambda *shape: pltpu.VMEM(shape, BF16)
    vf = lambda *shape: pltpu.VMEM(shape, F32)
    wkv_shape = (2 * HD // LANES, feats, heads, LANES) if heads > 1 else w_kv.shape
    return pl.pallas_call(
        functools.partial(kernel, cfg),
        out_shape=jax.ShapeDtypeStruct((rounds, 2, batch * R, cols), BF16),
        in_specs=[sm, sm] + [hb] * 11,
        out_specs=pl.BlockSpec(memory_space=pltpu.VMEM),
        scratch_shapes=[
            vb(rounds * batch * R, feats),
            vf(*key_scales.shape),
            vf(*value_scales.shape),
            vb(*queries_draft.shape),
            vb(*queries_verify.shape),
            vb(*wkv_shape),
            vb(*w_out.shape),
            vb(pairs, S, HD),
            vb(pairs, S, HD),
            vb(pairs, S, HD),
            vb(pairs, S, HD),
            vf(rows1, S),
            vf(rows1, S),
            vf(rows1, LANES),
            vf(rows1, LANES),
            vb(group * toks, batch * rows1),
            vf(pairs, fpad, 2 * HD),
            vf(n, fpad, 2 * HD),
            vb(2, pairs, rows1, HD),
            vb(2, n, rows1, HD),
            vf(2, pairs, 1, LANES),
            vf(2, n, 1, LANES),
            vb(2, pairs, rows1, HD),
            vb(2, toks, half),
            vb(2, toks, half),
            vb(2, ys, toks, half),
            vb(2, toks, half),
            vb(2, toks, half),
            dma(6 + 2 * HD // LANES), dma(4, pairs), dma(n), dma(n), dma(2, n), dma(2, n), dma(2, n), dma(2, n),
            dma(2, pairs), dma(pairs), dma(2, pairs), dma(2), dma(2), dma(2, ys), dma(2, ys), dma(2), dma(2),
        ],
        compiler_params=pltpu.CompilerParams(
            collective_id=0, has_side_effects=True, vmem_limit_bytes=58 * 1024 * 1024),
    )(lengths, accepted, hidden_new.reshape(rounds * batch * R, feats), key_scales, value_scales, queries_draft,
      queries_verify, w_kv, w_out, keys_cache, values_cache,
      key_levels, value_levels)


def solution(mesh):
    return jax.shard_map(
        functools.partial(per_device, mesh.shape["seq"], mesh.shape["tp"]),
        mesh=mesh,
        in_specs=(
            P(None, None, "seq"),
            P("seq", "tp", None),
            P("tp", "seq"),
            P(None, None, "tp", None, None),
            P(None, None, "tp", None, None),
            P(None, "tp", "seq", None),
            P(None, "tp", "seq", None),
            P(None, "tp", "seq", None),
            P(None, "tp", "seq", None),
            P(None, "tp", "seq"),
            P(None, "tp", "seq"),
            P(),
            P(),
        ),
        out_specs=P(None, None, None, "seq"),
        check_vma=False,
    )
```

```python
import functools
import math

import jax
import jax.numpy as jnp
from jax import lax
from jax.experimental import pallas as pl
from jax.experimental.pallas import tpu as pltpu
from jax.sharding import PartitionSpec as P

NEG = -1e30
AHEAD = 3
LANES = 128
F32 = jnp.float32
BF16 = jnp.bfloat16
MESH = pl.DeviceIdType.MESH


def onehot(rows, cols, source):
    r = lax.broadcasted_iota(jnp.int32, (rows, cols), 0)
    c = lax.broadcasted_iota(jnp.int32, (rows, cols), 1)
    return (source(r) == c).astype(F32).astype(BF16)


def kernel(cfg, *refs):
    (len_s, acc_s, hid_h, ks_h, vs_h, qd_h, qv_h, wkv_h, wout_h, k_h, v_h, kl_h, vl_h, out_ref,
     hid_v, ks_v, vs_v, qd_v, qv_v, wkv, wout, kc, vc, kl, vl, lk_a, lk_b, sc_a, sc_b, m_a, m_b, sel,
     fr_send, fr_recv, o_send, o_recv, st_send, st_recv, ag,
     rs_send, rs_recv, y_buf, fin_send, fin_recv,
     in_sem, kv_sem, frs_sem, frr_sem, os_sem, or_sem, ss_sem, sr_sem,
     ags_sem, agf_sem, agr_sem, rss_sem, rsr_sem, ys_sem, yr_sem, fs_sem, ffr_sem) = refs
    n, tp, batch, heads, rounds, R, group, S, HD, CH = cfg
    pairs = batch * heads
    k = n // pairs
    rows1 = rounds * group * R
    fpad = fr_send.shape[1]
    feats = hid_v.shape[1]
    ys = tp // 2
    me = lax.axis_index("seq")
    tpi = lax.axis_index("tp")
    mine = lax.div(me, k)
    sub = lax.rem(me, k)
    core = lax.rem(tpi, 2)
    sib = tpi + 1 - 2 * core
    yi = lax.div(tpi, 2)
    DRAFT, VERIFY = 0, 1

    barrier = pltpu.get_barrier_semaphore()
    for j in range(1, n):
        pl.semaphore_signal(barrier, inc=1, device_id={"seq": lax.rem(me + j, n)}, device_id_type=MESH)
    pl.semaphore_signal(barrier, inc=1, device_id={"tp": sib}, device_id_type=MESH)
    y_peers = [lax.rem(yi + j, ys) for j in range(1, ys)]
    for y in y_peers:
        pl.semaphore_signal(barrier, inc=1, device_id={"tp": 2 * y + core}, device_id_type=MESH)

    split_w = heads > 1
    if split_w:
        cp_wkv = [
            pltpu.make_async_copy(wkv_h.at[:, :, c * LANES:(c + 1) * LANES], wkv.at[c], in_sem.at[c])
            for c in range(2 * HD // LANES)
        ]
    else:
        cp_wkv = [pltpu.make_async_copy(wkv_h, wkv, in_sem.at[0])]
    base = 2 * HD // LANES
    cp_hid, cp_ks, cp_vs, cp_qd, cp_qv, cp_wout = [
        pltpu.make_async_copy(s, d, in_sem.at[base + j])
        for j, (s, d) in enumerate(((hid_h, hid_v), (ks_h, ks_v), (vs_h, vs_v), (qd_h, qd_v), (qv_h, qv_v),
                                    (wout_h, wout)))
    ]

    def place_of(u):
        return lax.rem(mine + 1 + u, pairs)

    def cache_copies(kind, p):
        b = lax.div(p, heads)
        h = lax.rem(p, heads)
        arrays = ((kl_h, kl), (vl_h, vl)) if kind == DRAFT else ((k_h, kc), (v_h, vc))
        return [
            pltpu.make_async_copy(src.at[b, h], dst.at[p], kv_sem.at[2 * kind + j, p])
            for j, (src, dst) in enumerate(arrays)
        ]

    def load_unit(kind, u):
        for c in cache_copies(kind, place_of(u)):
            c.start()

    ahead = min(AHEAD, pairs)
    cp_hid.start()
    for c in cp_wkv:
        c.start()
    cp_qd.start()
    cp_ks.start()
    cp_vs.start()
    for u in range(ahead):
        load_unit(DRAFT, u)

    tok = rounds * batch * R

    def fresh_source(r):
        b, q = r // fpad, r % fpad
        return jnp.where(q < rounds * R, (q // R) * (batch * R) + b * R + q % R, tok)

    frows = batch * fpad
    cp_hid.wait()
    hid = jnp.dot(onehot(frows, tok, fresh_source), hid_v[...], preferred_element_type=F32).astype(BF16)
    if split_w:
        blocks = feats // LANES
        stack = jnp.concatenate([hid[:, j * LANES:(j + 1) * LANES] for j in range(blocks)], axis=0)
        lhs = []
        for h in range(heads):
            r = lax.broadcasted_iota(jnp.int32, (LANES, heads * LANES), 0)
            c = lax.broadcasted_iota(jnp.int32, (LANES, heads * LANES), 1)
            spread = (heads * r + h == c).astype(F32).astype(BF16)
            wide = jnp.dot(stack, spread, preferred_element_type=F32).astype(BF16)
            lhs.append(jnp.concatenate([wide[j * frows:(j + 1) * frows] for j in range(blocks)], axis=1))
        lhs = jnp.concatenate(lhs, axis=0)
        for c, cp in enumerate(cp_wkv):
            cp.wait()
            part = jnp.dot(lhs, wkv[c].reshape(feats * heads, LANES), preferred_element_type=F32)
            for p in range(pairs):
                b, h = p // heads, p % heads
                fr_send[p, :, c * LANES:(c + 1) * LANES] = part[h * frows + b * fpad:h * frows + (b + 1) * fpad]
    else:
        cp_wkv[0].wait()
        part = jnp.dot(hid, wkv[:, 0, :], preferred_element_type=F32)
        for b in range(batch):
            fr_send[b] = part[b * fpad:(b + 1) * fpad]

    def fresh_copy(dst, slot):
        return pltpu.make_async_remote_copy(
            src_ref=fr_send.at[lax.div(dst, k)], dst_ref=fr_recv.at[slot],
            send_sem=frs_sem.at[dst], recv_sem=frr_sem.at[slot],
            device_id={"seq": dst}, device_id_type=MESH)

    fr_recv[me] = fr_send[mine]

    toks = rounds * batch * R

    def sel_source(r):
        g, q = r // toks, r % toks
        t, q = q // (batch * R), q % (batch * R)
        return (q // R) * rows1 + t * (group * R) + g * R + q % R

    sel[...] = onehot(group * toks, batch * rows1, sel_source)

    factor = (1.0 / math.sqrt(HD)) * math.log2(math.e)
    eye = (lax.broadcasted_iota(jnp.int32, (LANES, LANES), 0)
           == lax.broadcasted_iota(jnp.int32, (LANES, LANES), 1))[:rows1]

    def to_row(full):
        return jnp.sum(jnp.where(eye, full, 0.0), axis=0, keepdims=True)

    per = CH // LANES
    chunks = S // CH

    def scale_row(r, u):
        p = place_of(u)
        b, h = lax.div(p, heads), lax.rem(p, heads)
        return jnp.where(h == 0, r[b, 0:1, :], r[b, heads - 1:heads, :])

    def dequant(u, lk):
        p = place_of(u)
        row = scale_row(ks_v, u)
        cut = [row[:, c * LANES:(c + 1) * LANES] for c in range(S // LANES)]
        cut += [cut[0]] * (-len(cut) % 8)
        scales = jnp.concatenate(cut, axis=0).T
        for c in range(S // LANES):
            sl = slice(c * LANES, (c + 1) * LANES)
            lk[sl] = (kl[p, sl].astype(F32) * scales[:, c:c + 1]).astype(BF16)

    def score(kind, u, sc, m_ref, lk=None):
        p = place_of(u)
        b, h = lax.div(p, heads), lax.rem(p, heads)
        count = len_s[b] - me * S
        q = (qd_v if kind == DRAFT else qv_v)[:, b, h].reshape(rows1, HD)
        top = None
        for c in range(chunks):
            keys = lk[c * CH:(c + 1) * CH] if kind == DRAFT else kc[p, c * CH:(c + 1) * CH]
            s = lax.dot_general(q, keys, (((1,), (1,)), ((), ())), preferred_element_type=F32)
            s = jnp.where(lax.broadcasted_iota(jnp.int32, (1, CH), 1) + c * CH < count, s, NEG)
            sc[:, c * CH:(c + 1) * CH] = s
            for j in range(per):
                piece = s[:, j * LANES:(j + 1) * LANES]
                top = piece if top is None else jnp.maximum(top, piece)
        m = jnp.max(top, axis=1, keepdims=True) * factor
        m_ref[...] = jnp.broadcast_to(m, (rows1, LANES))

    def weigh(kind, u, sc, m_ref, o_dst, st_dst):
        p = place_of(u)
        count = len_s[lax.div(p, heads)] - me * S
        m = m_ref[...]
        acc = None
        if kind == DRAFT:
            row = scale_row(vs_v, u)
            l = None
            for c in range(chunks):
                parts = []
                for j in range(c * per, (c + 1) * per):
                    sl = slice(j * LANES, (j + 1) * LANES)
                    w = jnp.exp2(sc[:, sl] * factor - m)
                    l = w if l is None else l + w
                    parts.append((w * row[:, sl]).astype(BF16))
                one = jnp.dot(jnp.concatenate(parts, axis=1), vl[p, c * CH:(c + 1) * CH], preferred_element_type=F32)
                acc = one if acc is None else acc + one
            l = jnp.broadcast_to(jnp.sum(l, axis=1, keepdims=True), l.shape)
        else:
            for c in range(chunks):
                w = jnp.concatenate(
                    [jnp.exp2(sc[:, j * LANES:(j + 1) * LANES] * factor - m).astype(BF16)
                     for j in range(c * per, (c + 1) * per)], axis=1)
                values = jnp.concatenate([vc[p, c * CH:(c + 1) * CH], jnp.ones((CH, LANES), BF16)], axis=1)
                both = jnp.dot(w, values, preferred_element_type=F32)
                acc = both if acc is None else acc + both
            acc, l = acc[:, :HD], acc[:, HD:]
        o_dst[...] = (acc / l).astype(BF16)
        lse = to_row(m + jnp.log2(l))
        st_dst[...] = jnp.where(jnp.full(lse.shape, count) > 0, lse, NEG)

    def o_copy(kind, p, dst, slot, src):
        return pltpu.make_async_remote_copy(
            src_ref=src, dst_ref=o_recv.at[kind, slot], send_sem=os_sem.at[kind, dst],
            recv_sem=or_sem.at[kind, slot], device_id={"seq": dst}, device_id_type=MESH)

    def s_copy(kind, p, dst, slot, src):
        return pltpu.make_async_remote_copy(
            src_ref=src, dst_ref=st_recv.at[kind, slot], send_sem=ss_sem.at[kind, dst],
            recv_sem=sr_sem.at[kind, slot], device_id={"seq": dst}, device_id_type=MESH)

    def send_pair(kind, u):
        p = place_of(u)
        for e in range(k):
            dst = p * k + lax.rem(sub + e, k)
            o_copy(kind, p, dst, me, o_send.at[kind, p]).start()
            s_copy(kind, p, dst, me, st_send.at[kind, p]).start()

    def send_mine(kind):
        for e in range(1, k):
            dst = mine * k + lax.rem(sub + e, k)
            o_copy(kind, mine, dst, me, o_recv.at[kind, me]).start()
            s_copy(kind, mine, dst, me, st_recv.at[kind, me]).start()

    def arrived(kind, u):
        for c in cache_copies(kind, place_of(u)):
            c.wait()
        nxt = u + ahead
        if isinstance(nxt, int):
            if nxt < pairs:
                load_unit(kind, nxt)
            elif kind == DRAFT:
                load_unit(VERIFY, nxt - pairs)
        else:
            @pl.when(nxt < pairs)
            def _():
                load_unit(kind, nxt)

            if kind == DRAFT:
                @pl.when(nxt >= pairs)
                def _():
                    load_unit(VERIFY, nxt - pairs)

    def both_to(kind, u):
        p = place_of(u)
        return o_send.at[kind, p], st_send.at[kind, p]

    bm = lax.div(mine, heads)
    hm = lax.rem(mine, heads)

    def fresh_part(kind):
        total = fr_recv[0]
        for j in range(1, n):
            total = total + fr_recv[j]
        new_k = total[:, :HD].astype(BF16)
        new_v = total[:, HD:].astype(BF16)
        r_id = lax.broadcasted_iota(jnp.int32, (rows1, fpad), 0)
        c_id = lax.broadcasted_iota(jnp.int32, (rows1, fpad), 1)
        turn, i_q = r_id // (group * R), r_id % R
        c_turn, c_j = c_id // R, c_id % R
        limit = jnp.zeros((rows1, fpad), jnp.int32)
        for t in range(rounds - 1):
            limit = jnp.where(c_turn == t, acc_s[t, bm], limit)
        see = ((c_turn < turn) & (c_j < limit)) | ((c_turn == turn) & (c_j <= i_q))
        q = (qd_v if kind == DRAFT else qv_v)[:, bm, hm].reshape(rows1, HD)
        s = lax.dot_general(q, new_k, (((1,), (1,)), ((), ())), preferred_element_type=F32)
        s = jnp.where(see, s, NEG)
        m = jnp.max(s, axis=1, keepdims=True) * factor
        w = jnp.exp2(s * factor - m).astype(BF16)
        both = jnp.dot(w, jnp.concatenate([new_v, jnp.ones(new_v.shape, BF16)], axis=1), preferred_element_type=F32)
        l = both[:, HD:]
        return to_row(m + jnp.log2(l)), both[:, :HD] / l

    def combine(kind):
        row, o_new = fresh_part(kind)
        for j in range(1, n):
            src = lax.rem(me + j, n)
            o_copy(kind, mine, src, src, o_send.at[kind, 0]).wait_recv()
            s_copy(kind, mine, src, src, st_send.at[kind, 0]).wait_recv()
        lse = jnp.concatenate([row] + [st_recv[kind, j] for j in range(n)] + [jnp.full(row.shape, NEG)] * (-(n + 1) % 8),
                              axis=0)
        w = jnp.exp2(lse - jnp.max(lse, axis=0, keepdims=True))
        w = (w / jnp.sum(w, axis=0, keepdims=True)).T
        total = o_new * w[:rows1, 0:1]
        for j in range(n):
            total = total + o_recv[kind, j].astype(F32) * w[:rows1, j + 1:j + 2]
        ag[kind, mine] = total.astype(BF16)

    partner = mine + 1 - 2 * lax.rem(mine, 2)
    others = [lax.rem(mine + 2 * j, pairs) for j in range(1, pairs // 2)]
    across = [lax.rem(partner + 2 * j, pairs) for j in range(1, pairs // 2)]
    order = sorted(range(len(others)), key=lambda j: abs(j + 1 - pairs / 4))

    def ag_copy(kind, slot, to, sem):
        return pltpu.make_async_remote_copy(
            src_ref=ag.at[kind, slot], dst_ref=ag.at[kind, slot], send_sem=sem, recv_sem=agr_sem.at[kind, slot],
            device_id={"seq": to * k + sub}, device_id_type=MESH)

    def spread_rows(kind, direct):
        for j in order:
            ag_copy(kind, mine, others[j], ags_sem.at[kind, others[j]]).start()
        ag_copy(kind, mine, partner, ags_sem.at[kind, partner]).start()
        if direct:
            for q in across:
                ag_copy(kind, mine, q, ags_sem.at[kind, q]).start()

    far = [others[j] for j in reversed(order)]

    def forward_rows(kind):
        for q in far:
            ag_copy(kind, q, partner, agf_sem.at[q]).wait_recv()
            ag_copy(kind, q, partner, agf_sem.at[q]).start()

    def gathered(kind, direct):
        for q in ([partner] + across) + (others if direct else []):
            ag_copy(kind, q, partner, agf_sem.at[q]).wait_recv()

    last = pairs - 1
    hold = min(1, pairs // 2 - 2)

    cp_qd.wait()
    cp_ks.wait()
    cp_vs.wait()
    arrived(DRAFT, 0)
    dequant(0, lk_a)
    score(DRAFT, 0, sc_a, m_a, lk_a)

    @pl.loop(0, pairs // 2 - 1)
    def _(i):
        u = 2 * i
        arrived(DRAFT, u + 1)
        dequant(u + 1, lk_b)
        score(DRAFT, u + 1, sc_b, m_b, lk_b)
        weigh(DRAFT, u, sc_a, m_a, *both_to(DRAFT, u))
        arrived(DRAFT, u + 2)
        dequant(u + 2, lk_a)
        score(DRAFT, u + 2, sc_a, m_a, lk_a)
        weigh(DRAFT, u + 1, sc_b, m_b, *both_to(DRAFT, u + 1))

        @pl.when(i == hold)
        def _():
            pl.semaphore_wait(barrier, n - 1 + ys)
            for j in range(1, n):
                fresh_copy(lax.rem(me + j, n), me).start()
            for v in range(2 * hold):
                send_pair(DRAFT, v)

        @pl.when(i >= hold)
        def _():
            send_pair(DRAFT, u)
            send_pair(DRAFT, u + 1)

    arrived(DRAFT, last)
    cp_qv.start()
    dequant(last, lk_b)
    score(DRAFT, last, sc_b, m_b, lk_b)
    weigh(DRAFT, last - 1, sc_a, m_a, *both_to(DRAFT, last - 1))
    send_pair(DRAFT, last - 1)
    cp_qv.wait()
    arrived(VERIFY, 0)
    score(VERIFY, 0, sc_a, m_a)
    weigh(DRAFT, last, sc_b, m_b, o_recv.at[DRAFT, me], st_recv.at[DRAFT, me])
    send_mine(DRAFT)

    @pl.loop(0, pairs // 2 - 1)
    def _(i):
        u = 2 * i
        arrived(VERIFY, u + 1)
        score(VERIFY, u + 1, sc_b, m_b)
        weigh(VERIFY, u, sc_a, m_a, *both_to(VERIFY, u))
        send_pair(VERIFY, u)
        arrived(VERIFY, u + 2)
        score(VERIFY, u + 2, sc_a, m_a)
        weigh(VERIFY, u + 1, sc_b, m_b, *both_to(VERIFY, u + 1))
        send_pair(VERIFY, u + 1)

    arrived(VERIFY, last)
    cp_wout.start()
    score(VERIFY, last, sc_b, m_b)
    weigh(VERIFY, last - 1, sc_a, m_a, *both_to(VERIFY, last - 1))
    send_pair(VERIFY, last - 1)
    weigh(VERIFY, last, sc_b, m_b, o_recv.at[VERIFY, me], st_recv.at[VERIFY, me])
    send_mine(VERIFY)

    for j in range(1, n):
        fresh_copy(lax.rem(me + j, n), lax.rem(me + j, n)).wait_recv()
    combine(DRAFT)
    spread_rows(DRAFT, False)
    combine(VERIFY)
    spread_rows(VERIFY, True)
    forward_rows(DRAFT)

    depth = group * HD
    half = rs_send.shape[2]

    def lhs_of(kind):
        out = []
        for h in range(heads):
            rows = jnp.concatenate([ag[kind, b * heads + h] for b in range(batch)], axis=0)
            y = jnp.dot(sel[...], rows, preferred_element_type=F32)
            out.append(jnp.concatenate([y[g * toks:(g + 1) * toks] for g in range(group)], axis=1).astype(BF16))
        return out

    def columns(c):
        return pl.ds(pl.multiple_of(c * half, LANES), half)

    def project(lhs, c):
        acc = jnp.dot(lhs[0], wout[0:depth, columns(c)], preferred_element_type=F32)
        for h in range(1, heads):
            acc += jnp.dot(lhs[h], wout[h * depth:(h + 1) * depth, columns(c)], preferred_element_type=F32)
        return acc

    def rs_copy(kind):
        return pltpu.make_async_remote_copy(
            src_ref=rs_send.at[kind], dst_ref=rs_recv.at[kind], send_sem=rss_sem.at[kind],
            recv_sem=rsr_sem.at[kind], device_id={"tp": sib}, device_id_type=MESH)

    def y_copy(kind, slot, to):
        return pltpu.make_async_remote_copy(
            src_ref=y_buf.at[kind, slot], dst_ref=y_buf.at[kind, slot], send_sem=ys_sem.at[kind, to],
            recv_sem=yr_sem.at[kind, slot], device_id={"tp": 2 * to + core}, device_id_type=MESH)

    def fin_copy(kind):
        return pltpu.make_async_remote_copy(
            src_ref=fin_send.at[kind], dst_ref=fin_recv.at[kind], send_sem=fs_sem.at[kind],
            recv_sem=ffr_sem.at[kind], device_id={"tp": sib}, device_id_type=MESH)

    def first_sum(kind):
        lhs = lhs_of(kind)
        rs_send[kind] = project(lhs, 1 - core).astype(BF16)
        rs_copy(kind).start()
        return project(lhs, core)

    def second_sum(kind, own):
        rs_copy(kind).wait_recv()
        y_buf[kind, yi] = (own + rs_recv[kind].astype(F32)).astype(BF16)
        for y in y_peers:
            y_copy(kind, yi, y).start()

    def put(kind, c, value):
        out_ref[:, kind, :, columns(c)] = value.reshape(rounds, batch * R, half)

    def third_sum(kind):
        for y in y_peers:
            y_copy(kind, y, y).wait_recv()
        total = y_buf[kind, 0].astype(F32)
        for y in range(1, ys):
            total = total + y_buf[kind, y].astype(F32)
        total = total.astype(BF16)
        fin_send[kind] = total
        fin_copy(kind).start()
        put(kind, core, total)

    def finish(kind):
        fin_copy(kind).wait_recv()
        put(kind, 1 - core, fin_recv[kind])

    cp_wout.wait()
    gathered(DRAFT, False)
    own_d = first_sum(DRAFT)
    second_sum(DRAFT, own_d)
    gathered(VERIFY, True)
    own_v = first_sum(VERIFY)
    third_sum(DRAFT)
    second_sum(VERIFY, own_v)
    finish(DRAFT)
    third_sum(VERIFY)
    finish(VERIFY)

    for j in range(1, n):
        dst = lax.rem(me + j, n)
        fresh_copy(dst, me).wait_send()
        for kind in (DRAFT, VERIFY):
            o_copy(kind, 0, dst, me, o_send.at[kind, 0]).wait_send()
            s_copy(kind, 0, dst, me, st_send.at[kind, 0]).wait_send()
    for kind in (DRAFT, VERIFY):
        for q in others + [partner] + (across if kind == VERIFY else []):
            ag_copy(kind, mine, q, ags_sem.at[kind, q]).wait_send()
        rs_copy(kind).wait_send()
        fin_copy(kind).wait_send()
        for y in y_peers:
            y_copy(kind, yi, y).wait_send()
    for q in far:
        ag_copy(DRAFT, q, partner, agf_sem.at[q]).wait_send()


def per_device(n, tp, hidden_new, w_kv, w_out, queries_draft, queries_verify, keys_cache,
               values_cache, key_levels, value_levels, key_scales, value_scales, lengths, accepted):
    batch, heads, S, HD = keys_cache.shape
    rounds = hidden_new.shape[0]
    R = hidden_new.shape[1] // batch
    group = queries_draft.shape[3] // R
    pairs = batch * heads
    feats = hidden_new.shape[2]
    cols = w_out.shape[1]
    rows1 = rounds * group * R
    toks = rounds * batch * R
    fpad = -(-rounds * R // 16) * 16
    half = cols // 2
    ys = tp // 2
    chunk = 2 * LANES
    cfg = (n, tp, batch, heads, rounds, R, group, S, HD, chunk)
    sm = pl.BlockSpec(memory_space=pltpu.SMEM)
    hb = pl.BlockSpec(memory_space=pltpu.HBM)
    dma = lambda *shape: pltpu.SemaphoreType.DMA(shape)
    vb = lambda *shape: pltpu.VMEM(shape, BF16)
    vf = lambda *shape: pltpu.VMEM(shape, F32)
    wkv_shape = (2 * HD // LANES, feats, heads, LANES) if heads > 1 else w_kv.shape
    return pl.pallas_call(
        functools.partial(kernel, cfg),
        out_shape=pltpu.VMEM((rounds, 2, batch * R, cols), BF16),
        in_specs=[sm, sm] + [hb] * 11,
        out_specs=pl.BlockSpec(memory_space=pltpu.VMEM),
        scratch_shapes=[
            vb(rounds * batch * R, feats),
            vf(*key_scales.shape),
            vf(*value_scales.shape),
            vb(*queries_draft.shape),
            vb(*queries_verify.shape),
            vb(*wkv_shape),
            vb(*w_out.shape),
            vb(pairs, S, HD),
            vb(pairs, S, HD),
            vb(pairs, S, HD),
            vb(pairs, S, HD),
            vb(S, HD),
            vb(S, HD),
            vf(rows1, S),
            vf(rows1, S),
            vf(rows1, LANES),
            vf(rows1, LANES),
            vb(group * toks, batch * rows1),
            vf(pairs, fpad, 2 * HD),
            vf(n, fpad, 2 * HD),
            vb(2, pairs, rows1, HD),
            vb(2, n, rows1, HD),
            vf(2, pairs, 1, LANES),
            vf(2, n, 1, LANES),
            vb(2, pairs, rows1, HD),
            vb(2, toks, half),
            vb(2, toks, half),
            vb(2, ys, toks, half),
            vb(2, toks, half),
            vb(2, toks, half),
            dma(6 + 2 * HD // LANES), dma(4, pairs), dma(n), dma(n), dma(2, n), dma(2, n), dma(2, n), dma(2, n),
            dma(2, pairs), dma(pairs), dma(2, pairs), dma(2), dma(2), dma(2, ys), dma(2, ys), dma(2), dma(2),
        ],
        compiler_params=pltpu.CompilerParams(
            collective_id=0, has_side_effects=True, vmem_limit_bytes=58 * 1024 * 1024),
    )(lengths, accepted, hidden_new.reshape(rounds * batch * R, feats), key_scales, value_scales, queries_draft,
      queries_verify, w_kv, w_out, keys_cache, values_cache,
      key_levels, value_levels)


def solution(mesh):
    return jax.shard_map(
        functools.partial(per_device, mesh.shape["seq"], mesh.shape["tp"]),
        mesh=mesh,
        in_specs=(
            P(None, None, "seq"),
            P("seq", "tp", None),
            P("tp", "seq"),
            P(None, None, "tp", None, None),
            P(None, None, "tp", None, None),
            P(None, "tp", "seq", None),
            P(None, "tp", "seq", None),
            P(None, "tp", "seq", None),
            P(None, "tp", "seq", None),
            P(None, "tp", "seq"),
            P(None, "tp", "seq"),
            P(),
            P(),
        ),
        out_specs=P(None, None, None, "seq"),
        check_vma=False,
    )
```

```python
import functools
import math

import jax
import jax.numpy as jnp
from jax import lax
from jax.experimental import pallas as pl
from jax.experimental.pallas import tpu as pltpu
from jax.sharding import PartitionSpec as P

NEG = -1e30
AHEAD = 3
LANES = 128
F32 = jnp.float32
BF16 = jnp.bfloat16
MESH = pl.DeviceIdType.MESH


def onehot(rows, cols, source):
    r = lax.broadcasted_iota(jnp.int32, (rows, cols), 0)
    c = lax.broadcasted_iota(jnp.int32, (rows, cols), 1)
    return (source(r) == c).astype(F32).astype(BF16)


def kernel(cfg, *refs):
    (len_s, acc_s, hid_h, ks_h, vs_h, qd_h, qv_h, wkv_h, wout_h, k_h, v_h, kl_h, vl_h, out_ref,
     hid_v, ks_v, vs_v, qd_v, qv_v, wkv, wout, kc, vc, kl, vl, lk_a, lk_b, sc_a, sc_b, m_a, m_b, sel,
     fr_send, fr_recv, o_send, o_recv, st_send, st_recv, ag,
     rs_send, rs_recv, y_buf, fin_send, fin_recv,
     in_sem, kv_sem, frs_sem, frr_sem, os_sem, or_sem, ss_sem, sr_sem,
     ags_sem, agf_sem, agr_sem, rss_sem, rsr_sem, ys_sem, yr_sem, fs_sem, ffr_sem) = refs
    n, tp, batch, heads, rounds, R, group, S, HD, CH = cfg
    pairs = batch * heads
    k = n // pairs
    rows1 = rounds * group * R
    fpad = fr_send.shape[1]
    feats = hid_v.shape[1]
    ys = tp // 2
    me = lax.axis_index("seq")
    tpi = lax.axis_index("tp")
    mine = lax.div(me, k)
    sub = lax.rem(me, k)
    core = lax.rem(tpi, 2)
    sib = tpi + 1 - 2 * core
    yi = lax.div(tpi, 2)
    DRAFT, VERIFY = 0, 1

    barrier = pltpu.get_barrier_semaphore()
    for j in range(1, n):
        pl.semaphore_signal(barrier, inc=1, device_id={"seq": lax.rem(me + j, n)}, device_id_type=MESH)
    pl.semaphore_signal(barrier, inc=1, device_id={"tp": sib}, device_id_type=MESH)
    y_peers = [lax.rem(yi + j, ys) for j in range(1, ys)]
    for y in y_peers:
        pl.semaphore_signal(barrier, inc=1, device_id={"tp": 2 * y + core}, device_id_type=MESH)

    split_w = heads > 1
    if split_w:
        cp_wkv = [
            pltpu.make_async_copy(wkv_h.at[:, :, c * LANES:(c + 1) * LANES], wkv.at[c], in_sem.at[c])
            for c in range(2 * HD // LANES)
        ]
    else:
        cp_wkv = [pltpu.make_async_copy(wkv_h, wkv, in_sem.at[0])]
    base = 2 * HD // LANES
    cp_hid, cp_ks, cp_vs, cp_qd, cp_qv, cp_wout = [
        pltpu.make_async_copy(s, d, in_sem.at[base + j])
        for j, (s, d) in enumerate(((hid_h, hid_v), (ks_h, ks_v), (vs_h, vs_v), (qd_h, qd_v), (qv_h, qv_v),
                                    (wout_h, wout)))
    ]

    def place_of(u):
        return lax.rem(mine + 1 + u, pairs)

    def cache_copies(kind, p):
        b = lax.div(p, heads)
        h = lax.rem(p, heads)
        arrays = ((kl_h, kl), (vl_h, vl)) if kind == DRAFT else ((k_h, kc), (v_h, vc))
        return [
            pltpu.make_async_copy(src.at[b, h], dst.at[p], kv_sem.at[2 * kind + j, p])
            for j, (src, dst) in enumerate(arrays)
        ]

    def load_unit(kind, u):
        for c in cache_copies(kind, place_of(u)):
            c.start()

    ahead = min(AHEAD, pairs)
    cp_hid.start()
    for c in cp_wkv:
        c.start()
    cp_qd.start()
    cp_ks.start()
    cp_vs.start()
    for u in range(ahead):
        load_unit(DRAFT, u)

    tok = rounds * batch * R

    def fresh_source(r):
        b, q = r // fpad, r % fpad
        return jnp.where(q < rounds * R, (q // R) * (batch * R) + b * R + q % R, tok)

    frows = batch * fpad
    cp_hid.wait()
    hid = jnp.dot(onehot(frows, tok, fresh_source), hid_v[...], preferred_element_type=F32).astype(BF16)
    if split_w:
        blocks = feats // LANES
        stack = jnp.concatenate([hid[:, j * LANES:(j + 1) * LANES] for j in range(blocks)], axis=0)
        lhs = []
        for h in range(heads):
            r = lax.broadcasted_iota(jnp.int32, (LANES, heads * LANES), 0)
            c = lax.broadcasted_iota(jnp.int32, (LANES, heads * LANES), 1)
            spread = (heads * r + h == c).astype(F32).astype(BF16)
            wide = jnp.dot(stack, spread, preferred_element_type=F32).astype(BF16)
            lhs.append(jnp.concatenate([wide[j * frows:(j + 1) * frows] for j in range(blocks)], axis=1))
        lhs = jnp.concatenate(lhs, axis=0)
        for c, cp in enumerate(cp_wkv):
            cp.wait()
            part = jnp.dot(lhs, wkv[c].reshape(feats * heads, LANES), preferred_element_type=F32)
            for p in range(pairs):
                b, h = p // heads, p % heads
                fr_send[p, :, c * LANES:(c + 1) * LANES] = part[h * frows + b * fpad:h * frows + (b + 1) * fpad]
    else:
        cp_wkv[0].wait()
        part = jnp.dot(hid, wkv[:, 0, :], preferred_element_type=F32)
        for b in range(batch):
            fr_send[b] = part[b * fpad:(b + 1) * fpad]

    def fresh_copy(dst, slot):
        return pltpu.make_async_remote_copy(
            src_ref=fr_send.at[lax.div(dst, k)], dst_ref=fr_recv.at[slot],
            send_sem=frs_sem.at[dst], recv_sem=frr_sem.at[slot],
            device_id={"seq": dst}, device_id_type=MESH)

    fr_recv[me] = fr_send[mine]

    toks = rounds * batch * R

    def sel_source(r):
        g, q = r // toks, r % toks
        t, q = q // (batch * R), q % (batch * R)
        return (q // R) * rows1 + t * (group * R) + g * R + q % R


    sel[...] = onehot(group * toks, batch * rows1, sel_source)

    factor = (1.0 / math.sqrt(HD)) * math.log2(math.e)
    eye = (lax.broadcasted_iota(jnp.int32, (LANES, LANES), 0)
           == lax.broadcasted_iota(jnp.int32, (LANES, LANES), 1))[:rows1]

    def to_row(full):
        return jnp.sum(jnp.where(eye, full, 0.0), axis=0, keepdims=True)

    per = CH // LANES
    chunks = S // CH

    def scale_row(r, u):
        p = place_of(u)
        b, h = lax.div(p, heads), lax.rem(p, heads)
        return jnp.where(h == 0, r[b, 0:1, :], r[b, heads - 1:heads, :])

    def dequant(u, lk):
        p = place_of(u)
        row = scale_row(ks_v, u)
        cut = [row[:, c * LANES:(c + 1) * LANES] for c in range(S // LANES)]
        cut += [cut[0]] * (-len(cut) % 8)
        scales = jnp.concatenate(cut, axis=0).T
        for c in range(S // LANES):
            sl = slice(c * LANES, (c + 1) * LANES)
            lk[sl] = (kl[p, sl].astype(F32) * scales[:, c:c + 1]).astype(BF16)

    def score(kind, u, sc, m_ref, lk=None):
        p = place_of(u)
        b, h = lax.div(p, heads), lax.rem(p, heads)
        count = len_s[b] - me * S
        q = (qd_v if kind == DRAFT else qv_v)[:, b, h].reshape(rows1, HD)
        top = None
        for c in range(chunks):
            keys = lk[c * CH:(c + 1) * CH] if kind == DRAFT else kc[p, c * CH:(c + 1) * CH]
            s = lax.dot_general(q, keys, (((1,), (1,)), ((), ())), preferred_element_type=F32)
            s = jnp.where(lax.broadcasted_iota(jnp.int32, (1, CH), 1) + c * CH < count, s, NEG)
            sc[:, c * CH:(c + 1) * CH] = s
            for j in range(per):
                piece = s[:, j * LANES:(j + 1) * LANES]
                top = piece if top is None else jnp.maximum(top, piece)
        m = jnp.max(top, axis=1, keepdims=True) * factor
        m_ref[...] = jnp.broadcast_to(m, (rows1, LANES))

    def weigh(kind, u, sc, m_ref, o_dst, st_dst):
        p = place_of(u)
        count = len_s[lax.div(p, heads)] - me * S
        m = m_ref[...]
        acc = None
        if kind == DRAFT:
            row = scale_row(vs_v, u)
            l = None
            for c in range(chunks):
                parts = []
                for j in range(c * per, (c + 1) * per):
                    sl = slice(j * LANES, (j + 1) * LANES)
                    w = jnp.exp2(sc[:, sl] * factor - m)
                    l = w if l is None else l + w
                    parts.append((w * row[:, sl]).astype(BF16))
                one = jnp.dot(jnp.concatenate(parts, axis=1), vl[p, c * CH:(c + 1) * CH], preferred_element_type=F32)
                acc = one if acc is None else acc + one
            l = jnp.broadcast_to(jnp.sum(l, axis=1, keepdims=True), l.shape)
        else:
            for c in range(chunks):
                w = jnp.concatenate(
                    [jnp.exp2(sc[:, j * LANES:(j + 1) * LANES] * factor - m).astype(BF16)
                     for j in range(c * per, (c + 1) * per)], axis=1)
                values = jnp.concatenate([vc[p, c * CH:(c + 1) * CH], jnp.ones((CH, LANES), BF16)], axis=1)
                both = jnp.dot(w, values, preferred_element_type=F32)
                acc = both if acc is None else acc + both
            acc, l = acc[:, :HD], acc[:, HD:]
        o_dst[...] = (acc / l).astype(BF16)
        lse = to_row(m + jnp.log2(l))
        st_dst[...] = jnp.where(jnp.full(lse.shape, count) > 0, lse, NEG)

    def o_copy(kind, p, dst, slot, src):
        return pltpu.make_async_remote_copy(
            src_ref=src, dst_ref=o_recv.at[kind, slot], send_sem=os_sem.at[kind, dst],
            recv_sem=or_sem.at[kind, slot], device_id={"seq": dst}, device_id_type=MESH)

    def s_copy(kind, p, dst, slot, src):
        return pltpu.make_async_remote_copy(
            src_ref=src, dst_ref=st_recv.at[kind, slot], send_sem=ss_sem.at[kind, dst],
            recv_sem=sr_sem.at[kind, slot], device_id={"seq": dst}, device_id_type=MESH)

    def send_pair(kind, u):
        p = place_of(u)
        for e in range(k):
            dst = p * k + lax.rem(sub + e, k)
            o_copy(kind, p, dst, me, o_send.at[kind, p]).start()
            s_copy(kind, p, dst, me, st_send.at[kind, p]).start()

    def send_mine(kind):
        for e in range(1, k):
            dst = mine * k + lax.rem(sub + e, k)
            o_copy(kind, mine, dst, me, o_recv.at[kind, me]).start()
            s_copy(kind, mine, dst, me, st_recv.at[kind, me]).start()

    def arrived(kind, u):
        for c in cache_copies(kind, place_of(u)):
            c.wait()
        nxt = u + ahead
        if isinstance(nxt, int):
            if nxt < pairs:
                load_unit(kind, nxt)
            elif kind == DRAFT:
                load_unit(VERIFY, nxt - pairs)
        else:
            @pl.when(nxt < pairs)
            def _():
                load_unit(kind, nxt)

            if kind == DRAFT:
                @pl.when(nxt >= pairs)
                def _():
                    load_unit(VERIFY, nxt - pairs)

    def both_to(kind, u):
        p = place_of(u)
        return o_send.at[kind, p], st_send.at[kind, p]

    bm = lax.div(mine, heads)
    hm = lax.rem(mine, heads)

    def fresh_part(kind):
        total = fr_recv[0]
        for j in range(1, n):
            total = total + fr_recv[j]
        new_k = total[:, :HD].astype(BF16)
        new_v = total[:, HD:].astype(BF16)
        r_id = lax.broadcasted_iota(jnp.int32, (rows1, fpad), 0)
        c_id = lax.broadcasted_iota(jnp.int32, (rows1, fpad), 1)
        turn, i_q = r_id // (group * R), r_id % R
        c_turn, c_j = c_id // R, c_id % R
        limit = jnp.zeros((rows1, fpad), jnp.int32)
        for t in range(rounds - 1):
            limit = jnp.where(c_turn == t, acc_s[t, bm], limit)
        see = ((c_turn < turn) & (c_j < limit)) | ((c_turn == turn) & (c_j <= i_q))
        q = (qd_v if kind == DRAFT else qv_v)[:, bm, hm].reshape(rows1, HD)
        s = lax.dot_general(q, new_k, (((1,), (1,)), ((), ())), preferred_element_type=F32)
        s = jnp.where(see, s, NEG)
        m = jnp.max(s, axis=1, keepdims=True) * factor
        w = jnp.exp2(s * factor - m).astype(BF16)
        both = jnp.dot(w, jnp.concatenate([new_v, jnp.ones(new_v.shape, BF16)], axis=1), preferred_element_type=F32)
        l = both[:, HD:]
        return to_row(m + jnp.log2(l)), both[:, :HD] / l

    def combine(kind):
        row, o_new = fresh_part(kind)
        for j in range(1, n):
            src = lax.rem(me + j, n)
            o_copy(kind, mine, src, src, o_send.at[kind, 0]).wait_recv()
            s_copy(kind, mine, src, src, st_send.at[kind, 0]).wait_recv()
        lse = jnp.concatenate([row] + [st_recv[kind, j] for j in range(n)] + [jnp.full(row.shape, NEG)] * (-(n + 1) % 8),
                              axis=0)
        w = jnp.exp2(lse - jnp.max(lse, axis=0, keepdims=True))
        w = (w / jnp.sum(w, axis=0, keepdims=True)).T
        total = o_new * w[:rows1, 0:1]
        for j in range(n):
            total = total + o_recv[kind, j].astype(F32) * w[:rows1, j + 1:j + 2]
        ag[kind, mine] = total.astype(BF16)

    partner = mine + 1 - 2 * lax.rem(mine, 2)
    others = [lax.rem(mine + 2 * j, pairs) for j in range(1, pairs // 2)]
    across = [lax.rem(partner + 2 * j, pairs) for j in range(1, pairs // 2)]
    order = sorted(range(len(others)), key=lambda j: abs(j + 1 - pairs / 4))

    def ag_copy(kind, slot, to, sem):
        return pltpu.make_async_remote_copy(
            src_ref=ag.at[kind, slot], dst_ref=ag.at[kind, slot], send_sem=sem, recv_sem=agr_sem.at[kind, slot],
            device_id={"seq": to * k + sub}, device_id_type=MESH)

    def spread_rows(kind, direct):
        for j in order:
            ag_copy(kind, mine, others[j], ags_sem.at[kind, others[j]]).start()
        ag_copy(kind, mine, partner, ags_sem.at[kind, partner]).start()
        if direct:
            for q in across:
                ag_copy(kind, mine, q, ags_sem.at[kind, q]).start()

    far = [others[j] for j in reversed(order)]

    def forward_rows(kind):
        for q in far:
            ag_copy(kind, q, partner, agf_sem.at[q]).wait_recv()
            ag_copy(kind, q, partner, agf_sem.at[q]).start()

    def gathered(kind, direct):
        for q in ([partner] + across) + (others if direct else []):
            ag_copy(kind, q, partner, agf_sem.at[q]).wait_recv()

    last = pairs - 1

    cp_qd.wait()
    cp_ks.wait()
    cp_vs.wait()
    arrived(DRAFT, 0)
    dequant(0, lk_a)
    score(DRAFT, 0, sc_a, m_a, lk_a)

    @pl.loop(0, pairs // 2 - 1)
    def _(i):
        u = 2 * i
        arrived(DRAFT, u + 1)
        dequant(u + 1, lk_b)
        score(DRAFT, u + 1, sc_b, m_b, lk_b)
        weigh(DRAFT, u, sc_a, m_a, *both_to(DRAFT, u))
        arrived(DRAFT, u + 2)
        dequant(u + 2, lk_a)
        score(DRAFT, u + 2, sc_a, m_a, lk_a)
        weigh(DRAFT, u + 1, sc_b, m_b, *both_to(DRAFT, u + 1))

        @pl.when(i == 0)
        def _():
            pl.semaphore_wait(barrier, n - 1 + ys)
            for j in range(1, n):
                fresh_copy(lax.rem(me + j, n), me).start()

        send_pair(DRAFT, u)
        send_pair(DRAFT, u + 1)

    arrived(DRAFT, last)
    cp_qv.start()
    dequant(last, lk_b)
    score(DRAFT, last, sc_b, m_b, lk_b)
    weigh(DRAFT, last - 1, sc_a, m_a, *both_to(DRAFT, last - 1))
    send_pair(DRAFT, last - 1)
    cp_qv.wait()
    arrived(VERIFY, 0)
    score(VERIFY, 0, sc_a, m_a)
    weigh(DRAFT, last, sc_b, m_b, o_recv.at[DRAFT, me], st_recv.at[DRAFT, me])
    send_mine(DRAFT)

    @pl.loop(0, pairs // 2 - 1)
    def _(i):
        u = 2 * i
        arrived(VERIFY, u + 1)
        score(VERIFY, u + 1, sc_b, m_b)
        weigh(VERIFY, u, sc_a, m_a, *both_to(VERIFY, u))
        send_pair(VERIFY, u)
        arrived(VERIFY, u + 2)
        score(VERIFY, u + 2, sc_a, m_a)
        weigh(VERIFY, u + 1, sc_b, m_b, *both_to(VERIFY, u + 1))
        send_pair(VERIFY, u + 1)

    arrived(VERIFY, last)
    cp_wout.start()
    score(VERIFY, last, sc_b, m_b)
    weigh(VERIFY, last - 1, sc_a, m_a, *both_to(VERIFY, last - 1))
    send_pair(VERIFY, last - 1)
    weigh(VERIFY, last, sc_b, m_b, o_recv.at[VERIFY, me], st_recv.at[VERIFY, me])
    send_mine(VERIFY)

    for j in range(1, n):
        fresh_copy(lax.rem(me + j, n), lax.rem(me + j, n)).wait_recv()
    combine(DRAFT)
    spread_rows(DRAFT, False)
    combine(VERIFY)
    spread_rows(VERIFY, True)
    forward_rows(DRAFT)

    depth = group * HD
    half = rs_send.shape[2]

    def lhs_of(kind):
        out = []
        for h in range(heads):
            rows = jnp.concatenate([ag[kind, b * heads + h] for b in range(batch)], axis=0)
            y = jnp.dot(sel[...], rows, preferred_element_type=F32)
            out.append(jnp.concatenate([y[g * toks:(g + 1) * toks] for g in range(group)], axis=1).astype(BF16))
        return out

    def columns(c):
        return pl.ds(pl.multiple_of(c * half, LANES), half)

    def project(lhs, c):
        acc = jnp.dot(lhs[0], wout[0:depth, columns(c)], preferred_element_type=F32)
        for h in range(1, heads):
            acc += jnp.dot(lhs[h], wout[h * depth:(h + 1) * depth, columns(c)], preferred_element_type=F32)
        return acc

    def rs_copy(kind):
        return pltpu.make_async_remote_copy(
            src_ref=rs_send.at[kind], dst_ref=rs_recv.at[kind], send_sem=rss_sem.at[kind],
            recv_sem=rsr_sem.at[kind], device_id={"tp": sib}, device_id_type=MESH)

    def y_copy(kind, slot, to):
        return pltpu.make_async_remote_copy(
            src_ref=y_buf.at[kind, slot], dst_ref=y_buf.at[kind, slot], send_sem=ys_sem.at[kind, to],
            recv_sem=yr_sem.at[kind, slot], device_id={"tp": 2 * to + core}, device_id_type=MESH)

    def fin_copy(kind):
        return pltpu.make_async_remote_copy(
            src_ref=fin_send.at[kind], dst_ref=fin_recv.at[kind], send_sem=fs_sem.at[kind],
            recv_sem=ffr_sem.at[kind], device_id={"tp": sib}, device_id_type=MESH)

    def first_sum(kind):
        lhs = lhs_of(kind)
        rs_send[kind] = project(lhs, 1 - core).astype(BF16)
        rs_copy(kind).start()
        return project(lhs, core)

    def second_sum(kind, own):
        rs_copy(kind).wait_recv()
        y_buf[kind, yi] = (own + rs_recv[kind].astype(F32)).astype(BF16)
        for y in y_peers:
            y_copy(kind, yi, y).start()

    def put(kind, c, value):
        out_ref[:, kind, :, columns(c)] = value.reshape(rounds, batch * R, half)

    def third_sum(kind):
        for y in y_peers:
            y_copy(kind, y, y).wait_recv()
        total = y_buf[kind, 0].astype(F32)
        for y in range(1, ys):
            total = total + y_buf[kind, y].astype(F32)
        total = total.astype(BF16)
        fin_send[kind] = total
        fin_copy(kind).start()
        put(kind, core, total)

    def finish(kind):
        fin_copy(kind).wait_recv()
        put(kind, 1 - core, fin_recv[kind])

    cp_wout.wait()
    gathered(DRAFT, False)
    own_d = first_sum(DRAFT)
    second_sum(DRAFT, own_d)
    for j in range(1, n):
        dst = lax.rem(me + j, n)
        fresh_copy(dst, me).wait_send()
        for kind in (DRAFT, VERIFY):
            o_copy(kind, 0, dst, me, o_send.at[kind, 0]).wait_send()
            s_copy(kind, 0, dst, me, st_send.at[kind, 0]).wait_send()
    for q in others + [partner]:
        ag_copy(DRAFT, mine, q, ags_sem.at[DRAFT, q]).wait_send()
    gathered(VERIFY, True)
    own_v = first_sum(VERIFY)
    third_sum(DRAFT)
    second_sum(VERIFY, own_v)
    finish(DRAFT)
    for q in others + [partner] + across:
        ag_copy(VERIFY, mine, q, ags_sem.at[VERIFY, q]).wait_send()
    for q in far:
        ag_copy(DRAFT, q, partner, agf_sem.at[q]).wait_send()
    for kind in (DRAFT, VERIFY):
        rs_copy(kind).wait_send()
    fin_copy(DRAFT).wait_send()
    third_sum(VERIFY)
    for kind in (DRAFT, VERIFY):
        for y in y_peers:
            y_copy(kind, yi, y).wait_send()
    finish(VERIFY)
    fin_copy(VERIFY).wait_send()


def per_device(n, tp, hidden_new, w_kv, w_out, queries_draft, queries_verify, keys_cache,
               values_cache, key_levels, value_levels, key_scales, value_scales, lengths, accepted):
    batch, heads, S, HD = keys_cache.shape
    rounds = hidden_new.shape[0]
    R = hidden_new.shape[1] // batch
    group = queries_draft.shape[3] // R
    pairs = batch * heads
    feats = hidden_new.shape[2]
    cols = w_out.shape[1]
    rows1 = rounds * group * R
    toks = rounds * batch * R
    fpad = -(-rounds * R // 16) * 16
    half = cols // 2
    ys = tp // 2
    chunk = 2 * LANES
    cfg = (n, tp, batch, heads, rounds, R, group, S, HD, chunk)
    sm = pl.BlockSpec(memory_space=pltpu.SMEM)
    hb = pl.BlockSpec(memory_space=pltpu.HBM)
    dma = lambda *shape: pltpu.SemaphoreType.DMA(shape)
    vb = lambda *shape: pltpu.VMEM(shape, BF16)
    vf = lambda *shape: pltpu.VMEM(shape, F32)
    wkv_shape = (2 * HD // LANES, feats, heads, LANES) if heads > 1 else w_kv.shape
    return pl.pallas_call(
        functools.partial(kernel, cfg),
        out_shape=pltpu.VMEM((rounds, 2, batch * R, cols), BF16),
        in_specs=[sm, sm] + [hb] * 11,
        out_specs=pl.BlockSpec(memory_space=pltpu.VMEM),
        scratch_shapes=[
            vb(rounds * batch * R, feats),
            vf(*key_scales.shape),
            vf(*value_scales.shape),
            vb(*queries_draft.shape),
            vb(*queries_verify.shape),
            vb(*wkv_shape),
            vb(*w_out.shape),
            vb(pairs, S, HD),
            vb(pairs, S, HD),
            vb(pairs, S, HD),
            vb(pairs, S, HD),
            vb(S, HD),
            vb(S, HD),
            vf(rows1, S),
            vf(rows1, S),
            vf(rows1, LANES),
            vf(rows1, LANES),
            vb(group * toks, batch * rows1),
            vf(pairs, fpad, 2 * HD),
            vf(n, fpad, 2 * HD),
            vb(2, pairs, rows1, HD),
            vb(2, n, rows1, HD),
            vf(2, pairs, 1, LANES),
            vf(2, n, 1, LANES),
            vb(2, pairs, rows1, HD),
            vb(2, toks, half),
            vb(2, toks, half),
            vb(2, ys, toks, half),
            vb(2, toks, half),
            vb(2, toks, half),
            dma(6 + 2 * HD // LANES), dma(4, pairs), dma(n), dma(n), dma(2, n), dma(2, n), dma(2, n), dma(2, n),
            dma(2, pairs), dma(pairs), dma(2, pairs), dma(2), dma(2), dma(2, ys), dma(2, ys), dma(2), dma(2),
        ],
        compiler_params=pltpu.CompilerParams(
            collective_id=0, has_side_effects=True, vmem_limit_bytes=58 * 1024 * 1024),
    )(lengths, accepted, hidden_new.reshape(rounds * batch * R, feats), key_scales, value_scales, queries_draft,
      queries_verify, w_kv, w_out, keys_cache, values_cache,
      key_levels, value_levels)


def solution(mesh):
    return jax.shard_map(
        functools.partial(per_device, mesh.shape["seq"], mesh.shape["tp"]),
        mesh=mesh,
        in_specs=(
            P(None, None, "seq"),
            P("seq", "tp", None),
            P("tp", "seq"),
            P(None, None, "tp", None, None),
            P(None, None, "tp", None, None),
            P(None, "tp", "seq", None),
            P(None, "tp", "seq", None),
            P(None, "tp", "seq", None),
            P(None, "tp", "seq", None),
            P(None, "tp", "seq"),
            P(None, "tp", "seq"),
            P(),
            P(),
        ),
        out_specs=P(None, None, None, "seq"),
        check_vma=False,
    )
```

```python
import functools
import math

import jax
import jax.numpy as jnp
from jax import lax
from jax.experimental import pallas as pl
from jax.experimental.pallas import tpu as pltpu
from jax.sharding import PartitionSpec as P

NEG = -1e30
AHEAD = 3
LANES = 128
F32 = jnp.float32
BF16 = jnp.bfloat16
MESH = pl.DeviceIdType.MESH


def onehot(rows, cols, source):
    r = lax.broadcasted_iota(jnp.int32, (rows, cols), 0)
    c = lax.broadcasted_iota(jnp.int32, (rows, cols), 1)
    return (source(r) == c).astype(F32).astype(BF16)


def kernel(cfg, *refs):
    (len_s, acc_s, hid_h, ks_h, vs_h, qd_h, qv_h, wkv_h, wout_h, k_h, v_h, kl_h, vl_h, out_ref,
     hid_v, ks_v, vs_v, qd_v, qv_v, wkv, wout, kc, vc, kl, vl, lk_a, lk_b, sc_a, sc_b, m_a, m_b, sel,
     fr_send, fr_recv, o_send, o_recv, st_send, st_recv, ag,
     rs_send, rs_recv, y_buf, fin_send, fin_recv,
     in_sem, kv_sem, frs_sem, frr_sem, os_sem, or_sem, ss_sem, sr_sem,
     ags_sem, agf_sem, agr_sem, rss_sem, rsr_sem, ys_sem, yr_sem, fs_sem, ffr_sem) = refs
    n, tp, batch, heads, rounds, R, group, S, HD, CH = cfg
    pairs = batch * heads
    k = n // pairs
    rows1 = rounds * group * R
    fpad = fr_send.shape[1]
    feats = hid_v.shape[1]
    ys = tp // 2
    me = lax.axis_index("seq")
    tpi = lax.axis_index("tp")
    mine = lax.div(me, k)
    sub = lax.rem(me, k)
    core = lax.rem(tpi, 2)
    sib = tpi + 1 - 2 * core
    yi = lax.div(tpi, 2)
    DRAFT, VERIFY = 0, 1

    barrier = pltpu.get_barrier_semaphore()
    for j in range(1, n):
        pl.semaphore_signal(barrier, inc=1, device_id={"seq": lax.rem(me + j, n)}, device_id_type=MESH)
    pl.semaphore_signal(barrier, inc=1, device_id={"tp": sib}, device_id_type=MESH)
    y_peers = [lax.rem(yi + j, ys) for j in range(1, ys)]
    for y in y_peers:
        pl.semaphore_signal(barrier, inc=1, device_id={"tp": 2 * y + core}, device_id_type=MESH)

    split_w = heads > 1
    if split_w:
        cp_wkv = [
            pltpu.make_async_copy(wkv_h.at[:, :, c * LANES:(c + 1) * LANES], wkv.at[c], in_sem.at[c])
            for c in range(2 * HD // LANES)
        ]
    else:
        cp_wkv = [pltpu.make_async_copy(wkv_h, wkv, in_sem.at[0])]
    base = 2 * HD // LANES
    cp_hid, cp_ks, cp_vs, cp_qd, cp_qv, cp_wout = [
        pltpu.make_async_copy(s, d, in_sem.at[base + j])
        for j, (s, d) in enumerate(((hid_h, hid_v), (ks_h, ks_v), (vs_h, vs_v), (qd_h, qd_v), (qv_h, qv_v),
                                    (wout_h, wout)))
    ]

    def place_of(u):
        return lax.rem(mine + 1 + u, pairs)

    def cache_copies(kind, p):
        b = lax.div(p, heads)
        h = lax.rem(p, heads)
        arrays = ((kl_h, kl), (vl_h, vl)) if kind == DRAFT else ((k_h, kc), (v_h, vc))
        return [
            pltpu.make_async_copy(src.at[b, h], dst.at[p], kv_sem.at[2 * kind + j, p])
            for j, (src, dst) in enumerate(arrays)
        ]

    def load_unit(kind, u):
        for c in cache_copies(kind, place_of(u)):
            c.start()

    ahead = min(AHEAD, pairs)
    cp_hid.start()
    for c in cp_wkv:
        c.start()
    cp_qd.start()
    cp_ks.start()
    cp_vs.start()
    for u in range(ahead):
        load_unit(DRAFT, u)

    tok = rounds * batch * R

    def fresh_source(r):
        b, q = r // fpad, r % fpad
        return jnp.where(q < rounds * R, (q // R) * (batch * R) + b * R + q % R, tok)

    frows = batch * fpad
    cp_hid.wait()
    hid = jnp.dot(onehot(frows, tok, fresh_source), hid_v[...], preferred_element_type=F32).astype(BF16)
    if split_w:
        blocks = feats // LANES
        stack = jnp.concatenate([hid[:, j * LANES:(j + 1) * LANES] for j in range(blocks)], axis=0)
        lhs = []
        for h in range(heads):
            r = lax.broadcasted_iota(jnp.int32, (LANES, heads * LANES), 0)
            c = lax.broadcasted_iota(jnp.int32, (LANES, heads * LANES), 1)
            spread = (heads * r + h == c).astype(F32).astype(BF16)
            wide = jnp.dot(stack, spread, preferred_element_type=F32).astype(BF16)
            lhs.append(jnp.concatenate([wide[j * frows:(j + 1) * frows] for j in range(blocks)], axis=1))
        lhs = jnp.concatenate(lhs, axis=0)
        for c, cp in enumerate(cp_wkv):
            cp.wait()
            part = jnp.dot(lhs, wkv[c].reshape(feats * heads, LANES), preferred_element_type=F32)
            for p in range(pairs):
                b, h = p // heads, p % heads
                fr_send[p, :, c * LANES:(c + 1) * LANES] = part[h * frows + b * fpad:h * frows + (b + 1) * fpad]
    else:
        cp_wkv[0].wait()
        part = jnp.dot(hid, wkv[:, 0, :], preferred_element_type=F32)
        for b in range(batch):
            fr_send[b] = part[b * fpad:(b + 1) * fpad]

    def fresh_copy(dst, slot):
        return pltpu.make_async_remote_copy(
            src_ref=fr_send.at[lax.div(dst, k)], dst_ref=fr_recv.at[slot],
            send_sem=frs_sem.at[dst], recv_sem=frr_sem.at[slot],
            device_id={"seq": dst}, device_id_type=MESH)

    fr_recv[me] = fr_send[mine]

    toks = rounds * batch * R

    def sel_source(r):
        g, q = r // toks, r % toks
        t, q = q // (batch * R), q % (batch * R)
        return (q // R) * rows1 + t * (group * R) + g * R + q % R


    sel[...] = onehot(group * toks, batch * rows1, sel_source)

    factor = (1.0 / math.sqrt(HD)) * math.log2(math.e)
    eye = (lax.broadcasted_iota(jnp.int32, (LANES, LANES), 0)
           == lax.broadcasted_iota(jnp.int32, (LANES, LANES), 1))[:rows1]

    def to_row(full):
        return jnp.sum(jnp.where(eye, full, 0.0), axis=0, keepdims=True)

    per = CH // LANES
    chunks = S // CH

    def scale_row(r, u):
        p = place_of(u)
        b, h = lax.div(p, heads), lax.rem(p, heads)
        return jnp.where(h == 0, r[b, 0:1, :], r[b, heads - 1:heads, :])

    def dequant(u, lk):
        p = place_of(u)
        row = scale_row(ks_v, u)
        cut = [row[:, c * LANES:(c + 1) * LANES] for c in range(S // LANES)]
        cut += [cut[0]] * (-len(cut) % 8)
        scales = jnp.concatenate(cut, axis=0).T
        for c in range(S // LANES):
            sl = slice(c * LANES, (c + 1) * LANES)
            lk[sl] = (kl[p, sl].astype(F32) * scales[:, c:c + 1]).astype(BF16)

    def score(kind, u, sc, m_ref, lk=None):
        p = place_of(u)
        b, h = lax.div(p, heads), lax.rem(p, heads)
        count = len_s[b] - me * S
        q = (qd_v if kind == DRAFT else qv_v)[:, b, h].reshape(rows1, HD)
        top = None
        for c in range(chunks):
            keys = lk[c * CH:(c + 1) * CH] if kind == DRAFT else kc[p, c * CH:(c + 1) * CH]
            s = lax.dot_general(q, keys, (((1,), (1,)), ((), ())), preferred_element_type=F32)
            s = jnp.where(lax.broadcasted_iota(jnp.int32, (1, CH), 1) + c * CH < count, s, NEG)
            sc[:, c * CH:(c + 1) * CH] = s
            for j in range(per):
                piece = s[:, j * LANES:(j + 1) * LANES]
                top = piece if top is None else jnp.maximum(top, piece)
        m = jnp.max(top, axis=1, keepdims=True) * factor
        m_ref[...] = jnp.broadcast_to(m, (rows1, LANES))

    def weigh(kind, u, sc, m_ref, o_dst, st_dst):
        p = place_of(u)
        count = len_s[lax.div(p, heads)] - me * S
        m = m_ref[...]
        acc = None
        if kind == DRAFT:
            row = scale_row(vs_v, u)
            l = None
            for c in range(chunks):
                parts = []
                for j in range(c * per, (c + 1) * per):
                    sl = slice(j * LANES, (j + 1) * LANES)
                    w = jnp.exp2(sc[:, sl] * factor - m)
                    l = w if l is None else l + w
                    parts.append((w * row[:, sl]).astype(BF16))
                one = jnp.dot(jnp.concatenate(parts, axis=1), vl[p, c * CH:(c + 1) * CH], preferred_element_type=F32)
                acc = one if acc is None else acc + one
            l = jnp.broadcast_to(jnp.sum(l, axis=1, keepdims=True), l.shape)
        else:
            for c in range(chunks):
                w = jnp.concatenate(
                    [jnp.exp2(sc[:, j * LANES:(j + 1) * LANES] * factor - m).astype(BF16)
                     for j in range(c * per, (c + 1) * per)], axis=1)
                values = jnp.concatenate([vc[p, c * CH:(c + 1) * CH], jnp.ones((CH, LANES), BF16)], axis=1)
                both = jnp.dot(w, values, preferred_element_type=F32)
                acc = both if acc is None else acc + both
            acc, l = acc[:, :HD], acc[:, HD:]
        o_dst[...] = (acc / l).astype(BF16)
        lse = to_row(m + jnp.log2(l))
        st_dst[...] = jnp.where(jnp.full(lse.shape, count) > 0, lse, NEG)

    def o_copy(kind, p, dst, slot, src):
        return pltpu.make_async_remote_copy(
            src_ref=src, dst_ref=o_recv.at[kind, slot], send_sem=os_sem.at[kind, dst],
            recv_sem=or_sem.at[kind, slot], device_id={"seq": dst}, device_id_type=MESH)

    def s_copy(kind, p, dst, slot, src):
        return pltpu.make_async_remote_copy(
            src_ref=src, dst_ref=st_recv.at[kind, slot], send_sem=ss_sem.at[kind, dst],
            recv_sem=sr_sem.at[kind, slot], device_id={"seq": dst}, device_id_type=MESH)

    def send_pair(kind, u):
        p = place_of(u)
        for e in range(k):
            dst = p * k + lax.rem(sub + e, k)
            o_copy(kind, p, dst, me, o_send.at[kind, p]).start()
            s_copy(kind, p, dst, me, st_send.at[kind, p]).start()

    def send_mine(kind):
        for e in range(1, k):
            dst = mine * k + lax.rem(sub + e, k)
            o_copy(kind, mine, dst, me, o_recv.at[kind, me]).start()
            s_copy(kind, mine, dst, me, st_recv.at[kind, me]).start()

    def arrived(kind, u):
        for c in cache_copies(kind, place_of(u)):
            c.wait()
        nxt = u + ahead
        if isinstance(nxt, int):
            if nxt < pairs:
                load_unit(kind, nxt)
            elif kind == DRAFT:
                load_unit(VERIFY, nxt - pairs)
        else:
            @pl.when(nxt < pairs)
            def _():
                load_unit(kind, nxt)

            if kind == DRAFT:
                @pl.when(nxt >= pairs)
                def _():
                    load_unit(VERIFY, nxt - pairs)

    def both_to(kind, u):
        p = place_of(u)
        return o_send.at[kind, p], st_send.at[kind, p]

    bm = lax.div(mine, heads)
    hm = lax.rem(mine, heads)

    def fresh_part(kind):
        total = fr_recv[0]
        for j in range(1, n):
            total = total + fr_recv[j]
        new_k = total[:, :HD].astype(BF16)
        new_v = total[:, HD:].astype(BF16)
        r_id = lax.broadcasted_iota(jnp.int32, (rows1, fpad), 0)
        c_id = lax.broadcasted_iota(jnp.int32, (rows1, fpad), 1)
        turn, i_q = r_id // (group * R), r_id % R
        c_turn, c_j = c_id // R, c_id % R
        limit = jnp.zeros((rows1, fpad), jnp.int32)
        for t in range(rounds - 1):
            limit = jnp.where(c_turn == t, acc_s[t, bm], limit)
        see = ((c_turn < turn) & (c_j < limit)) | ((c_turn == turn) & (c_j <= i_q))
        q = (qd_v if kind == DRAFT else qv_v)[:, bm, hm].reshape(rows1, HD)
        s = lax.dot_general(q, new_k, (((1,), (1,)), ((), ())), preferred_element_type=F32)
        s = jnp.where(see, s, NEG)
        m = jnp.max(s, axis=1, keepdims=True) * factor
        w = jnp.exp2(s * factor - m).astype(BF16)
        both = jnp.dot(w, jnp.concatenate([new_v, jnp.ones(new_v.shape, BF16)], axis=1), preferred_element_type=F32)
        l = both[:, HD:]
        return to_row(m + jnp.log2(l)), both[:, :HD] / l

    def combine(kind):
        row, o_new = fresh_part(kind)
        for j in range(1, n):
            src = lax.rem(me + j, n)
            o_copy(kind, mine, src, src, o_send.at[kind, 0]).wait_recv()
            s_copy(kind, mine, src, src, st_send.at[kind, 0]).wait_recv()
        lse = jnp.concatenate([row] + [st_recv[kind, j] for j in range(n)] + [jnp.full(row.shape, NEG)] * (-(n + 1) % 8),
                              axis=0)
        w = jnp.exp2(lse - jnp.max(lse, axis=0, keepdims=True))
        w = (w / jnp.sum(w, axis=0, keepdims=True)).T
        total = o_new * w[:rows1, 0:1]
        for j in range(n):
            total = total + o_recv[kind, j].astype(F32) * w[:rows1, j + 1:j + 2]
        ag[kind, mine] = total.astype(BF16)

    partner = mine + 1 - 2 * lax.rem(mine, 2)
    others = [lax.rem(mine + 2 * j, pairs) for j in range(1, pairs // 2)]
    across = [lax.rem(partner + 2 * j, pairs) for j in range(1, pairs // 2)]
    order = sorted(range(len(others)), key=lambda j: abs(j + 1 - pairs / 4))

    def ag_copy(kind, slot, to, sem):
        return pltpu.make_async_remote_copy(
            src_ref=ag.at[kind, slot], dst_ref=ag.at[kind, slot], send_sem=sem, recv_sem=agr_sem.at[kind, slot],
            device_id={"seq": to * k + sub}, device_id_type=MESH)

    def spread_rows(kind, direct):
        for j in order:
            ag_copy(kind, mine, others[j], ags_sem.at[kind, others[j]]).start()
        ag_copy(kind, mine, partner, ags_sem.at[kind, partner]).start()
        if direct:
            for q in across:
                ag_copy(kind, mine, q, ags_sem.at[kind, q]).start()

    far = [others[j] for j in reversed(order)]

    def forward_rows(kind):
        for q in far:
            ag_copy(kind, q, partner, agf_sem.at[q]).wait_recv()
            ag_copy(kind, q, partner, agf_sem.at[q]).start()

    def gathered(kind, direct):
        for q in ([partner] + across) + (others if direct else []):
            ag_copy(kind, q, partner, agf_sem.at[q]).wait_recv()

    last = pairs - 1

    cp_qd.wait()
    cp_ks.wait()
    cp_vs.wait()
    arrived(DRAFT, 0)
    dequant(0, lk_a)
    score(DRAFT, 0, sc_a, m_a, lk_a)

    @pl.loop(0, pairs // 2 - 1)
    def _(i):
        u = 2 * i
        arrived(DRAFT, u + 1)
        dequant(u + 1, lk_b)
        score(DRAFT, u + 1, sc_b, m_b, lk_b)
        weigh(DRAFT, u, sc_a, m_a, *both_to(DRAFT, u))
        arrived(DRAFT, u + 2)
        dequant(u + 2, lk_a)
        score(DRAFT, u + 2, sc_a, m_a, lk_a)
        weigh(DRAFT, u + 1, sc_b, m_b, *both_to(DRAFT, u + 1))

        @pl.when(i == 0)
        def _():
            pl.semaphore_wait(barrier, n - 1 + ys)
            for j in range(1, n):
                fresh_copy(lax.rem(me + j, n), me).start()

        send_pair(DRAFT, u)
        send_pair(DRAFT, u + 1)

    arrived(DRAFT, last)
    cp_qv.start()
    dequant(last, lk_b)
    score(DRAFT, last, sc_b, m_b, lk_b)
    weigh(DRAFT, last - 1, sc_a, m_a, *both_to(DRAFT, last - 1))
    send_pair(DRAFT, last - 1)
    cp_qv.wait()
    arrived(VERIFY, 0)
    score(VERIFY, 0, sc_a, m_a)
    weigh(DRAFT, last, sc_b, m_b, o_recv.at[DRAFT, me], st_recv.at[DRAFT, me])
    send_mine(DRAFT)

    @pl.loop(0, pairs // 2 - 1)
    def _(i):
        u = 2 * i
        arrived(VERIFY, u + 1)
        score(VERIFY, u + 1, sc_b, m_b)
        weigh(VERIFY, u, sc_a, m_a, *both_to(VERIFY, u))
        send_pair(VERIFY, u)
        arrived(VERIFY, u + 2)
        score(VERIFY, u + 2, sc_a, m_a)
        weigh(VERIFY, u + 1, sc_b, m_b, *both_to(VERIFY, u + 1))
        send_pair(VERIFY, u + 1)

    arrived(VERIFY, last)
    cp_wout.start()
    score(VERIFY, last, sc_b, m_b)
    weigh(VERIFY, last - 1, sc_a, m_a, *both_to(VERIFY, last - 1))
    send_pair(VERIFY, last - 1)
    weigh(VERIFY, last, sc_b, m_b, o_recv.at[VERIFY, me], st_recv.at[VERIFY, me])
    send_mine(VERIFY)

    for j in range(1, n):
        fresh_copy(lax.rem(me + j, n), lax.rem(me + j, n)).wait_recv()
    combine(DRAFT)
    spread_rows(DRAFT, False)
    combine(VERIFY)
    spread_rows(VERIFY, True)
    forward_rows(DRAFT)

    depth = group * HD
    half = rs_send.shape[2]

    def lhs_of(kind):
        out = []
        for h in range(heads):
            rows = jnp.concatenate([ag[kind, b * heads + h] for b in range(batch)], axis=0)
            y = jnp.dot(sel[...], rows, preferred_element_type=F32)
            out.append(jnp.concatenate([y[g * toks:(g + 1) * toks] for g in range(group)], axis=1).astype(BF16))
        return out

    def columns(c):
        return pl.ds(pl.multiple_of(c * half, LANES), half)

    def project(lhs, c):
        acc = jnp.dot(lhs[0], wout[0:depth, columns(c)], preferred_element_type=F32)
        for h in range(1, heads):
            acc += jnp.dot(lhs[h], wout[h * depth:(h + 1) * depth, columns(c)], preferred_element_type=F32)
        return acc

    def rs_copy(kind):
        return pltpu.make_async_remote_copy(
            src_ref=rs_send.at[kind], dst_ref=rs_recv.at[kind], send_sem=rss_sem.at[kind],
            recv_sem=rsr_sem.at[kind], device_id={"tp": sib}, device_id_type=MESH)

    def y_copy(kind, slot, to):
        return pltpu.make_async_remote_copy(
            src_ref=y_buf.at[kind, slot], dst_ref=y_buf.at[kind, slot], send_sem=ys_sem.at[kind, to],
            recv_sem=yr_sem.at[kind, slot], device_id={"tp": 2 * to + core}, device_id_type=MESH)

    def fin_copy(kind):
        return pltpu.make_async_remote_copy(
            src_ref=fin_send.at[kind], dst_ref=fin_recv.at[kind], send_sem=fs_sem.at[kind],
            recv_sem=ffr_sem.at[kind], device_id={"tp": sib}, device_id_type=MESH)

    def first_sum(kind):
        lhs = lhs_of(kind)
        rs_send[kind] = project(lhs, 1 - core).astype(BF16)
        rs_copy(kind).start()
        return project(lhs, core)

    def second_sum(kind, own):
        rs_copy(kind).wait_recv()
        y_buf[kind, yi] = (own + rs_recv[kind].astype(F32)).astype(BF16)
        for y in y_peers:
            y_copy(kind, yi, y).start()

    def put(kind, c, value):
        out_ref[:, kind, :, columns(c)] = value.reshape(rounds, batch * R, half)

    def third_sum(kind):
        for y in y_peers:
            y_copy(kind, y, y).wait_recv()
        total = y_buf[kind, 0].astype(F32)
        for y in range(1, ys):
            total = total + y_buf[kind, y].astype(F32)
        total = total.astype(BF16)
        fin_send[kind] = total
        fin_copy(kind).start()
        put(kind, core, total)

    def finish(kind):
        fin_copy(kind).wait_recv()
        put(kind, 1 - core, fin_recv[kind])

    cp_wout.wait()
    gathered(DRAFT, False)
    own_d = first_sum(DRAFT)
    second_sum(DRAFT, own_d)
    for j in range(1, n):
        dst = lax.rem(me + j, n)
        fresh_copy(dst, me).wait_send()
        for kind in (DRAFT, VERIFY):
            o_copy(kind, 0, dst, me, o_send.at[kind, 0]).wait_send()
            s_copy(kind, 0, dst, me, st_send.at[kind, 0]).wait_send()
    for q in others + [partner]:
        ag_copy(DRAFT, mine, q, ags_sem.at[DRAFT, q]).wait_send()
    gathered(VERIFY, True)
    own_v = first_sum(VERIFY)
    second_sum(VERIFY, own_v)
    third_sum(DRAFT)
    finish(DRAFT)
    for q in others + [partner] + across:
        ag_copy(VERIFY, mine, q, ags_sem.at[VERIFY, q]).wait_send()
    for q in far:
        ag_copy(DRAFT, q, partner, agf_sem.at[q]).wait_send()
    for kind in (DRAFT, VERIFY):
        rs_copy(kind).wait_send()
    fin_copy(DRAFT).wait_send()
    third_sum(VERIFY)
    for kind in (DRAFT, VERIFY):
        for y in y_peers:
            y_copy(kind, yi, y).wait_send()
    finish(VERIFY)
    fin_copy(VERIFY).wait_send()


def per_device(n, tp, hidden_new, w_kv, w_out, queries_draft, queries_verify, keys_cache,
               values_cache, key_levels, value_levels, key_scales, value_scales, lengths, accepted):
    batch, heads, S, HD = keys_cache.shape
    rounds = hidden_new.shape[0]
    R = hidden_new.shape[1] // batch
    group = queries_draft.shape[3] // R
    pairs = batch * heads
    feats = hidden_new.shape[2]
    cols = w_out.shape[1]
    rows1 = rounds * group * R
    toks = rounds * batch * R
    fpad = -(-rounds * R // 16) * 16
    half = cols // 2
    ys = tp // 2
    chunk = 2 * LANES
    cfg = (n, tp, batch, heads, rounds, R, group, S, HD, chunk)
    sm = pl.BlockSpec(memory_space=pltpu.SMEM)
    hb = pl.BlockSpec(memory_space=pltpu.HBM)
    dma = lambda *shape: pltpu.SemaphoreType.DMA(shape)
    vb = lambda *shape: pltpu.VMEM(shape, BF16)
    vf = lambda *shape: pltpu.VMEM(shape, F32)
    wkv_shape = (2 * HD // LANES, feats, heads, LANES) if heads > 1 else w_kv.shape
    return pl.pallas_call(
        functools.partial(kernel, cfg),
        out_shape=pltpu.VMEM((rounds, 2, batch * R, cols), BF16),
        in_specs=[sm, sm] + [hb] * 11,
        out_specs=pl.BlockSpec(memory_space=pltpu.VMEM),
        scratch_shapes=[
            vb(rounds * batch * R, feats),
            vf(*key_scales.shape),
            vf(*value_scales.shape),
            vb(*queries_draft.shape),
            vb(*queries_verify.shape),
            vb(*wkv_shape),
            vb(*w_out.shape),
            vb(pairs, S, HD),
            vb(pairs, S, HD),
            vb(pairs, S, HD),
            vb(pairs, S, HD),
            vb(S, HD),
            vb(S, HD),
            vf(rows1, S),
            vf(rows1, S),
            vf(rows1, LANES),
            vf(rows1, LANES),
            vb(group * toks, batch * rows1),
            vf(pairs, fpad, 2 * HD),
            vf(n, fpad, 2 * HD),
            vb(2, pairs, rows1, HD),
            vb(2, n, rows1, HD),
            vf(2, pairs, 1, LANES),
            vf(2, n, 1, LANES),
            vb(2, pairs, rows1, HD),
            vb(2, toks, half),
            vb(2, toks, half),
            vb(2, ys, toks, half),
            vb(2, toks, half),
            vb(2, toks, half),
            dma(6 + 2 * HD // LANES), dma(4, pairs), dma(n), dma(n), dma(2, n), dma(2, n), dma(2, n), dma(2, n),
            dma(2, pairs), dma(pairs), dma(2, pairs), dma(2), dma(2), dma(2, ys), dma(2, ys), dma(2), dma(2),
        ],
        compiler_params=pltpu.CompilerParams(
            collective_id=0, has_side_effects=True, vmem_limit_bytes=58 * 1024 * 1024),
    )(lengths, accepted, hidden_new.reshape(rounds * batch * R, feats), key_scales, value_scales, queries_draft,
      queries_verify, w_kv, w_out, keys_cache, values_cache,
      key_levels, value_levels)


def solution(mesh):
    return jax.shard_map(
        functools.partial(per_device, mesh.shape["seq"], mesh.shape["tp"]),
        mesh=mesh,
        in_specs=(
            P(None, None, "seq"),
            P("seq", "tp", None),
            P("tp", "seq"),
            P(None, None, "tp", None, None),
            P(None, None, "tp", None, None),
            P(None, "tp", "seq", None),
            P(None, "tp", "seq", None),
            P(None, "tp", "seq", None),
            P(None, "tp", "seq", None),
            P(None, "tp", "seq"),
            P(None, "tp", "seq"),
            P(),
            P(),
        ),
        out_specs=P(None, None, None, "seq"),
        check_vma=False,
    )
```

```python
import functools
import math

import jax
import jax.numpy as jnp
from jax import lax
from jax.experimental import pallas as pl
from jax.experimental.pallas import tpu as pltpu
from jax.sharding import PartitionSpec as P

NEG = -1e30
AHEAD = 3
LANES = 128
F32 = jnp.float32
BF16 = jnp.bfloat16
MESH = pl.DeviceIdType.MESH


def onehot(rows, cols, source):
    r = lax.broadcasted_iota(jnp.int32, (rows, cols), 0)
    c = lax.broadcasted_iota(jnp.int32, (rows, cols), 1)
    return (source(r) == c).astype(F32).astype(BF16)


def kernel(cfg, *refs):
    (len_s, acc_s, hid_h, ks_h, vs_h, qd_h, qv_h, wkv_h, wout_h, k_h, v_h, kl_h, vl_h, out_ref,
     hid_v, ks_v, vs_v, qd_v, qv_v, wkv, wout, kc, vc, kl, vl, lk_a, lk_b, sc_a, sc_b, m_a, m_b, sel,
     fr_send, fr_recv, o_send, o_recv, st_send, st_recv, ag,
     rs_send, rs_recv, y_buf, fin_send, fin_recv,
     in_sem, kv_sem, frs_sem, frr_sem, os_sem, or_sem, ss_sem, sr_sem,
     ags_sem, agf_sem, agr_sem, rss_sem, rsr_sem, ys_sem, yr_sem, fs_sem, ffr_sem) = refs
    n, tp, batch, heads, rounds, R, group, S, HD, CH = cfg
    pairs = batch * heads
    k = n // pairs
    rows1 = rounds * group * R
    fpad = fr_send.shape[1]
    feats = hid_v.shape[1]
    ys = tp // 2
    me = lax.axis_index("seq")
    tpi = lax.axis_index("tp")
    mine = lax.div(me, k)
    sub = lax.rem(me, k)
    core = lax.rem(tpi, 2)
    sib = tpi + 1 - 2 * core
    yi = lax.div(tpi, 2)
    DRAFT, VERIFY = 0, 1

    barrier = pltpu.get_barrier_semaphore()
    for j in range(1, n):
        pl.semaphore_signal(barrier, inc=1, device_id={"seq": lax.rem(me + j, n)}, device_id_type=MESH)
    pl.semaphore_signal(barrier, inc=1, device_id={"tp": sib}, device_id_type=MESH)
    y_peers = [lax.rem(yi + j, ys) for j in range(1, ys)]
    for y in y_peers:
        pl.semaphore_signal(barrier, inc=1, device_id={"tp": 2 * y + core}, device_id_type=MESH)

    split_w = heads > 1
    if split_w:
        cp_wkv = [
            pltpu.make_async_copy(wkv_h.at[:, :, c * LANES:(c + 1) * LANES], wkv.at[c], in_sem.at[c])
            for c in range(2 * HD // LANES)
        ]
    else:
        cp_wkv = [pltpu.make_async_copy(wkv_h, wkv, in_sem.at[0])]
    base = 2 * HD // LANES
    cp_hid, cp_ks, cp_vs, cp_qd, cp_qv, cp_wout = [
        pltpu.make_async_copy(s, d, in_sem.at[base + j])
        for j, (s, d) in enumerate(((hid_h, hid_v), (ks_h, ks_v), (vs_h, vs_v), (qd_h, qd_v), (qv_h, qv_v),
                                    (wout_h, wout)))
    ]

    def place_of(u):
        return lax.rem(mine + 1 + u, pairs)

    def cache_copies(kind, p):
        b = lax.div(p, heads)
        h = lax.rem(p, heads)
        arrays = ((kl_h, kl), (vl_h, vl)) if kind == DRAFT else ((k_h, kc), (v_h, vc))
        return [
            pltpu.make_async_copy(src.at[b, h], dst.at[p], kv_sem.at[2 * kind + j, p])
            for j, (src, dst) in enumerate(arrays)
        ]

    def load_unit(kind, u):
        for c in cache_copies(kind, place_of(u)):
            c.start()

    ahead = min(AHEAD, pairs)
    cp_hid.start()
    for c in cp_wkv:
        c.start()
    cp_qd.start()
    cp_ks.start()
    cp_vs.start()
    for u in range(ahead):
        load_unit(DRAFT, u)

    tok = rounds * batch * R

    def fresh_source(r):
        b, q = r // fpad, r % fpad
        return jnp.where(q < rounds * R, (q // R) * (batch * R) + b * R + q % R, tok)

    frows = batch * fpad
    cp_hid.wait()
    hid = jnp.dot(onehot(frows, tok, fresh_source), hid_v[...], preferred_element_type=F32).astype(BF16)
    if split_w:
        blocks = feats // LANES
        stack = jnp.concatenate([hid[:, j * LANES:(j + 1) * LANES] for j in range(blocks)], axis=0)
        lhs = []
        for h in range(heads):
            r = lax.broadcasted_iota(jnp.int32, (LANES, heads * LANES), 0)
            c = lax.broadcasted_iota(jnp.int32, (LANES, heads * LANES), 1)
            spread = (heads * r + h == c).astype(F32).astype(BF16)
            wide = jnp.dot(stack, spread, preferred_element_type=F32).astype(BF16)
            lhs.append(jnp.concatenate([wide[j * frows:(j + 1) * frows] for j in range(blocks)], axis=1))
        lhs = jnp.concatenate(lhs, axis=0)
        for c, cp in enumerate(cp_wkv):
            cp.wait()
            part = jnp.dot(lhs, wkv[c].reshape(feats * heads, LANES), preferred_element_type=F32)
            for p in range(pairs):
                b, h = p // heads, p % heads
                fr_send[p, :, c * LANES:(c + 1) * LANES] = part[h * frows + b * fpad:h * frows + (b + 1) * fpad]
    else:
        cp_wkv[0].wait()
        part = jnp.dot(hid, wkv[:, 0, :], preferred_element_type=F32)
        for b in range(batch):
            fr_send[b] = part[b * fpad:(b + 1) * fpad]

    def fresh_copy(dst, slot):
        return pltpu.make_async_remote_copy(
            src_ref=fr_send.at[lax.div(dst, k)], dst_ref=fr_recv.at[slot],
            send_sem=frs_sem.at[dst], recv_sem=frr_sem.at[slot],
            device_id={"seq": dst}, device_id_type=MESH)

    fr_recv[me] = fr_send[mine]

    toks = rounds * batch * R

    def sel_source(r):
        g, q = r // toks, r % toks
        t, q = q // (batch * R), q % (batch * R)
        return (q // R) * rows1 + t * (group * R) + g * R + q % R


    sel[...] = onehot(group * toks, batch * rows1, sel_source)

    factor = (1.0 / math.sqrt(HD)) * math.log2(math.e)
    eye = (lax.broadcasted_iota(jnp.int32, (LANES, LANES), 0)
           == lax.broadcasted_iota(jnp.int32, (LANES, LANES), 1))[:rows1]

    def to_row(full):
        return jnp.sum(jnp.where(eye, full, 0.0), axis=0, keepdims=True)

    per = CH // LANES
    chunks = S // CH

    def scale_row(r, u):
        p = place_of(u)
        b, h = lax.div(p, heads), lax.rem(p, heads)
        return jnp.where(h == 0, r[b, 0:1, :], r[b, heads - 1:heads, :])

    def dequant(u, lk):
        p = place_of(u)
        row = scale_row(ks_v, u)
        cut = [row[:, c * LANES:(c + 1) * LANES] for c in range(S // LANES)]
        cut += [cut[0]] * (-len(cut) % 8)
        scales = jnp.concatenate(cut, axis=0).T
        for c in range(S // LANES):
            sl = slice(c * LANES, (c + 1) * LANES)
            lk[sl] = (kl[p, sl].astype(F32) * scales[:, c:c + 1]).astype(BF16)

    def score(kind, u, sc, m_ref, lk=None):
        p = place_of(u)
        b, h = lax.div(p, heads), lax.rem(p, heads)
        count = len_s[b] - me * S
        q = (qd_v if kind == DRAFT else qv_v)[:, b, h].reshape(rows1, HD)
        top = None
        for c in range(chunks):
            keys = lk[c * CH:(c + 1) * CH] if kind == DRAFT else kc[p, c * CH:(c + 1) * CH]
            s = lax.dot_general(q, keys, (((1,), (1,)), ((), ())), preferred_element_type=F32)
            s = jnp.where(lax.broadcasted_iota(jnp.int32, (1, CH), 1) + c * CH < count, s, NEG)
            sc[:, c * CH:(c + 1) * CH] = s
            for j in range(per):
                piece = s[:, j * LANES:(j + 1) * LANES]
                top = piece if top is None else jnp.maximum(top, piece)
        m = jnp.max(top, axis=1, keepdims=True) * factor
        m_ref[...] = jnp.broadcast_to(m, (rows1, LANES))

    def weigh(kind, u, sc, m_ref, o_dst, st_dst):
        p = place_of(u)
        count = len_s[lax.div(p, heads)] - me * S
        m = m_ref[...]
        acc = None
        if kind == DRAFT:
            row = scale_row(vs_v, u)
            l = None
            for c in range(chunks):
                parts = []
                for j in range(c * per, (c + 1) * per):
                    sl = slice(j * LANES, (j + 1) * LANES)
                    w = jnp.exp2(sc[:, sl] * factor - m)
                    l = w if l is None else l + w
                    parts.append((w * row[:, sl]).astype(BF16))
                one = jnp.dot(jnp.concatenate(parts, axis=1), vl[p, c * CH:(c + 1) * CH], preferred_element_type=F32)
                acc = one if acc is None else acc + one
            l = jnp.broadcast_to(jnp.sum(l, axis=1, keepdims=True), l.shape)
        else:
            l = None
            for c in range(chunks):
                parts = []
                for j in range(c * per, (c + 1) * per):
                    w = jnp.exp2(sc[:, j * LANES:(j + 1) * LANES] * factor - m).astype(BF16)
                    parts.append(w)
                    l = w.astype(F32) if l is None else l + w.astype(F32)
                one = jnp.dot(jnp.concatenate(parts, axis=1), vc[p, c * CH:(c + 1) * CH], preferred_element_type=F32)
                acc = one if acc is None else acc + one
            l = jnp.broadcast_to(jnp.sum(l, axis=1, keepdims=True), l.shape)
        o_dst[...] = (acc / l).astype(BF16)
        lse = to_row(m + jnp.log2(l))
        st_dst[...] = jnp.where(jnp.full(lse.shape, count) > 0, lse, NEG)

    def o_copy(kind, p, dst, slot, src):
        return pltpu.make_async_remote_copy(
            src_ref=src, dst_ref=o_recv.at[kind, slot], send_sem=os_sem.at[kind, dst],
            recv_sem=or_sem.at[kind, slot], device_id={"seq": dst}, device_id_type=MESH)

    def s_copy(kind, p, dst, slot, src):
        return pltpu.make_async_remote_copy(
            src_ref=src, dst_ref=st_recv.at[kind, slot], send_sem=ss_sem.at[kind, dst],
            recv_sem=sr_sem.at[kind, slot], device_id={"seq": dst}, device_id_type=MESH)

    def send_pair(kind, u):
        p = place_of(u)
        for e in range(k):
            dst = p * k + lax.rem(sub + e, k)
            o_copy(kind, p, dst, me, o_send.at[kind, p]).start()
            s_copy(kind, p, dst, me, st_send.at[kind, p]).start()

    def send_mine(kind):
        for e in range(1, k):
            dst = mine * k + lax.rem(sub + e, k)
            o_copy(kind, mine, dst, me, o_recv.at[kind, me]).start()
            s_copy(kind, mine, dst, me, st_recv.at[kind, me]).start()

    def arrived(kind, u):
        for c in cache_copies(kind, place_of(u)):
            c.wait()
        nxt = u + ahead
        if isinstance(nxt, int):
            if nxt < pairs:
                load_unit(kind, nxt)
            elif kind == DRAFT:
                load_unit(VERIFY, nxt - pairs)
        else:
            @pl.when(nxt < pairs)
            def _():
                load_unit(kind, nxt)

            if kind == DRAFT:
                @pl.when(nxt >= pairs)
                def _():
                    load_unit(VERIFY, nxt - pairs)

    def both_to(kind, u):
        p = place_of(u)
        return o_send.at[kind, p], st_send.at[kind, p]

    bm = lax.div(mine, heads)
    hm = lax.rem(mine, heads)

    def fresh_part(kind):
        total = fr_recv[0]
        for j in range(1, n):
            total = total + fr_recv[j]
        new_k = total[:, :HD].astype(BF16)
        new_v = total[:, HD:].astype(BF16)
        r_id = lax.broadcasted_iota(jnp.int32, (rows1, fpad), 0)
        c_id = lax.broadcasted_iota(jnp.int32, (rows1, fpad), 1)
        turn, i_q = r_id // (group * R), r_id % R
        c_turn, c_j = c_id // R, c_id % R
        limit = jnp.zeros((rows1, fpad), jnp.int32)
        for t in range(rounds - 1):
            limit = jnp.where(c_turn == t, acc_s[t, bm], limit)
        see = ((c_turn < turn) & (c_j < limit)) | ((c_turn == turn) & (c_j <= i_q))
        q = (qd_v if kind == DRAFT else qv_v)[:, bm, hm].reshape(rows1, HD)
        s = lax.dot_general(q, new_k, (((1,), (1,)), ((), ())), preferred_element_type=F32)
        s = jnp.where(see, s, NEG)
        m = jnp.max(s, axis=1, keepdims=True) * factor
        w = jnp.exp2(s * factor - m).astype(BF16)
        both = jnp.dot(w, jnp.concatenate([new_v, jnp.ones(new_v.shape, BF16)], axis=1), preferred_element_type=F32)
        l = both[:, HD:]
        return to_row(m + jnp.log2(l)), both[:, :HD] / l

    def combine(kind):
        row, o_new = fresh_part(kind)
        for j in range(1, n):
            src = lax.rem(me + j, n)
            o_copy(kind, mine, src, src, o_send.at[kind, 0]).wait_recv()
            s_copy(kind, mine, src, src, st_send.at[kind, 0]).wait_recv()
        lse = jnp.concatenate([row] + [st_recv[kind, j] for j in range(n)] + [jnp.full(row.shape, NEG)] * (-(n + 1) % 8),
                              axis=0)
        w = jnp.exp2(lse - jnp.max(lse, axis=0, keepdims=True))
        w = (w / jnp.sum(w, axis=0, keepdims=True)).T
        total = o_new * w[:rows1, 0:1]
        for j in range(n):
            total = total + o_recv[kind, j].astype(F32) * w[:rows1, j + 1:j + 2]
        ag[kind, mine] = total.astype(BF16)

    partner = mine + 1 - 2 * lax.rem(mine, 2)
    others = [lax.rem(mine + 2 * j, pairs) for j in range(1, pairs // 2)]
    across = [lax.rem(partner + 2 * j, pairs) for j in range(1, pairs // 2)]
    order = sorted(range(len(others)), key=lambda j: abs(j + 1 - pairs / 4))

    def ag_copy(kind, slot, to, sem):
        return pltpu.make_async_remote_copy(
            src_ref=ag.at[kind, slot], dst_ref=ag.at[kind, slot], send_sem=sem, recv_sem=agr_sem.at[kind, slot],
            device_id={"seq": to * k + sub}, device_id_type=MESH)

    def spread_rows(kind, direct):
        for j in order:
            ag_copy(kind, mine, others[j], ags_sem.at[kind, others[j]]).start()
        ag_copy(kind, mine, partner, ags_sem.at[kind, partner]).start()
        if direct:
            for q in across:
                ag_copy(kind, mine, q, ags_sem.at[kind, q]).start()

    far = [others[j] for j in reversed(order)]

    def forward_rows(kind):
        for q in far:
            ag_copy(kind, q, partner, agf_sem.at[q]).wait_recv()
            ag_copy(kind, q, partner, agf_sem.at[q]).start()

    def gathered(kind, direct):
        for q in ([partner] + across) + (others if direct else []):
            ag_copy(kind, q, partner, agf_sem.at[q]).wait_recv()

    last = pairs - 1

    cp_qd.wait()
    cp_ks.wait()
    cp_vs.wait()
    arrived(DRAFT, 0)
    dequant(0, lk_a)
    score(DRAFT, 0, sc_a, m_a, lk_a)

    @pl.loop(0, pairs // 2 - 1)
    def _(i):
        u = 2 * i
        arrived(DRAFT, u + 1)
        dequant(u + 1, lk_b)
        score(DRAFT, u + 1, sc_b, m_b, lk_b)
        weigh(DRAFT, u, sc_a, m_a, *both_to(DRAFT, u))
        arrived(DRAFT, u + 2)
        dequant(u + 2, lk_a)
        score(DRAFT, u + 2, sc_a, m_a, lk_a)
        weigh(DRAFT, u + 1, sc_b, m_b, *both_to(DRAFT, u + 1))

        @pl.when(i == 0)
        def _():
            pl.semaphore_wait(barrier, n - 1 + ys)
            for j in range(1, n):
                fresh_copy(lax.rem(me + j, n), me).start()

        send_pair(DRAFT, u)
        send_pair(DRAFT, u + 1)

    arrived(DRAFT, last)
    cp_qv.start()
    dequant(last, lk_b)
    score(DRAFT, last, sc_b, m_b, lk_b)
    weigh(DRAFT, last - 1, sc_a, m_a, *both_to(DRAFT, last - 1))
    send_pair(DRAFT, last - 1)
    cp_qv.wait()
    arrived(VERIFY, 0)
    score(VERIFY, 0, sc_a, m_a)
    weigh(DRAFT, last, sc_b, m_b, o_recv.at[DRAFT, me], st_recv.at[DRAFT, me])
    send_mine(DRAFT)

    @pl.loop(0, pairs // 2 - 1)
    def _(i):
        u = 2 * i
        arrived(VERIFY, u + 1)
        score(VERIFY, u + 1, sc_b, m_b)
        weigh(VERIFY, u, sc_a, m_a, *both_to(VERIFY, u))
        send_pair(VERIFY, u)
        arrived(VERIFY, u + 2)
        score(VERIFY, u + 2, sc_a, m_a)
        weigh(VERIFY, u + 1, sc_b, m_b, *both_to(VERIFY, u + 1))
        send_pair(VERIFY, u + 1)

    arrived(VERIFY, last)
    cp_wout.start()
    score(VERIFY, last, sc_b, m_b)
    weigh(VERIFY, last - 1, sc_a, m_a, *both_to(VERIFY, last - 1))
    send_pair(VERIFY, last - 1)
    weigh(VERIFY, last, sc_b, m_b, o_recv.at[VERIFY, me], st_recv.at[VERIFY, me])
    send_mine(VERIFY)

    for j in range(1, n):
        fresh_copy(lax.rem(me + j, n), lax.rem(me + j, n)).wait_recv()
    combine(DRAFT)
    spread_rows(DRAFT, False)
    combine(VERIFY)
    spread_rows(VERIFY, True)
    forward_rows(DRAFT)

    depth = group * HD
    half = rs_send.shape[2]

    def lhs_of(kind):
        out = []
        for h in range(heads):
            rows = jnp.concatenate([ag[kind, b * heads + h] for b in range(batch)], axis=0)
            y = jnp.dot(sel[...], rows, preferred_element_type=F32)
            out.append(jnp.concatenate([y[g * toks:(g + 1) * toks] for g in range(group)], axis=1).astype(BF16))
        return out

    def columns(c):
        return pl.ds(pl.multiple_of(c * half, LANES), half)

    def project(lhs, c):
        acc = jnp.dot(lhs[0], wout[0:depth, columns(c)], preferred_element_type=F32)
        for h in range(1, heads):
            acc += jnp.dot(lhs[h], wout[h * depth:(h + 1) * depth, columns(c)], preferred_element_type=F32)
        return acc

    def rs_copy(kind):
        return pltpu.make_async_remote_copy(
            src_ref=rs_send.at[kind], dst_ref=rs_recv.at[kind], send_sem=rss_sem.at[kind],
            recv_sem=rsr_sem.at[kind], device_id={"tp": sib}, device_id_type=MESH)

    def y_copy(kind, slot, to):
        return pltpu.make_async_remote_copy(
            src_ref=y_buf.at[kind, slot], dst_ref=y_buf.at[kind, slot], send_sem=ys_sem.at[kind, to],
            recv_sem=yr_sem.at[kind, slot], device_id={"tp": 2 * to + core}, device_id_type=MESH)

    def fin_copy(kind):
        return pltpu.make_async_remote_copy(
            src_ref=fin_send.at[kind], dst_ref=fin_recv.at[kind], send_sem=fs_sem.at[kind],
            recv_sem=ffr_sem.at[kind], device_id={"tp": sib}, device_id_type=MESH)

    def first_sum(kind):
        lhs = lhs_of(kind)
        rs_send[kind] = project(lhs, 1 - core).astype(BF16)
        rs_copy(kind).start()
        return project(lhs, core)

    def second_sum(kind, own):
        rs_copy(kind).wait_recv()
        y_buf[kind, yi] = (own + rs_recv[kind].astype(F32)).astype(BF16)
        for y in y_peers:
            y_copy(kind, yi, y).start()

    def put(kind, c, value):
        out_ref[:, kind, :, columns(c)] = value.reshape(rounds, batch * R, half)

    def third_sum(kind):
        for y in y_peers:
            y_copy(kind, y, y).wait_recv()
        total = y_buf[kind, 0].astype(F32)
        for y in range(1, ys):
            total = total + y_buf[kind, y].astype(F32)
        total = total.astype(BF16)
        fin_send[kind] = total
        fin_copy(kind).start()
        put(kind, core, total)

    def finish(kind):
        fin_copy(kind).wait_recv()
        put(kind, 1 - core, fin_recv[kind])

    cp_wout.wait()
    gathered(DRAFT, False)
    own_d = first_sum(DRAFT)
    second_sum(DRAFT, own_d)
    for j in range(1, n):
        dst = lax.rem(me + j, n)
        fresh_copy(dst, me).wait_send()
        for kind in (DRAFT, VERIFY):
            o_copy(kind, 0, dst, me, o_send.at[kind, 0]).wait_send()
            s_copy(kind, 0, dst, me, st_send.at[kind, 0]).wait_send()
    for q in others + [partner]:
        ag_copy(DRAFT, mine, q, ags_sem.at[DRAFT, q]).wait_send()
    gathered(VERIFY, True)
    own_v = first_sum(VERIFY)
    second_sum(VERIFY, own_v)
    third_sum(DRAFT)
    finish(DRAFT)
    for q in others + [partner] + across:
        ag_copy(VERIFY, mine, q, ags_sem.at[VERIFY, q]).wait_send()
    for q in far:
        ag_copy(DRAFT, q, partner, agf_sem.at[q]).wait_send()
    for kind in (DRAFT, VERIFY):
        rs_copy(kind).wait_send()
    fin_copy(DRAFT).wait_send()
    third_sum(VERIFY)
    for kind in (DRAFT, VERIFY):
        for y in y_peers:
            y_copy(kind, yi, y).wait_send()
    finish(VERIFY)
    fin_copy(VERIFY).wait_send()


def per_device(n, tp, hidden_new, w_kv, w_out, queries_draft, queries_verify, keys_cache,
               values_cache, key_levels, value_levels, key_scales, value_scales, lengths, accepted):
    batch, heads, S, HD = keys_cache.shape
    rounds = hidden_new.shape[0]
    R = hidden_new.shape[1] // batch
    group = queries_draft.shape[3] // R
    pairs = batch * heads
    feats = hidden_new.shape[2]
    cols = w_out.shape[1]
    rows1 = rounds * group * R
    toks = rounds * batch * R
    fpad = -(-rounds * R // 16) * 16
    half = cols // 2
    ys = tp // 2
    chunk = 2 * LANES
    cfg = (n, tp, batch, heads, rounds, R, group, S, HD, chunk)
    sm = pl.BlockSpec(memory_space=pltpu.SMEM)
    hb = pl.BlockSpec(memory_space=pltpu.HBM)
    dma = lambda *shape: pltpu.SemaphoreType.DMA(shape)
    vb = lambda *shape: pltpu.VMEM(shape, BF16)
    vf = lambda *shape: pltpu.VMEM(shape, F32)
    wkv_shape = (2 * HD // LANES, feats, heads, LANES) if heads > 1 else w_kv.shape
    return pl.pallas_call(
        functools.partial(kernel, cfg),
        out_shape=pltpu.VMEM((rounds, 2, batch * R, cols), BF16),
        in_specs=[sm, sm] + [hb] * 11,
        out_specs=pl.BlockSpec(memory_space=pltpu.VMEM),
        scratch_shapes=[
            vb(rounds * batch * R, feats),
            vf(*key_scales.shape),
            vf(*value_scales.shape),
            vb(*queries_draft.shape),
            vb(*queries_verify.shape),
            vb(*wkv_shape),
            vb(*w_out.shape),
            vb(pairs, S, HD),
            vb(pairs, S, HD),
            vb(pairs, S, HD),
            vb(pairs, S, HD),
            vb(S, HD),
            vb(S, HD),
            vf(rows1, S),
            vf(rows1, S),
            vf(rows1, LANES),
            vf(rows1, LANES),
            vb(group * toks, batch * rows1),
            vf(pairs, fpad, 2 * HD),
            vf(n, fpad, 2 * HD),
            vb(2, pairs, rows1, HD),
            vb(2, n, rows1, HD),
            vf(2, pairs, 1, LANES),
            vf(2, n, 1, LANES),
            vb(2, pairs, rows1, HD),
            vb(2, toks, half),
            vb(2, toks, half),
            vb(2, ys, toks, half),
            vb(2, toks, half),
            vb(2, toks, half),
            dma(6 + 2 * HD // LANES), dma(4, pairs), dma(n), dma(n), dma(2, n), dma(2, n), dma(2, n), dma(2, n),
            dma(2, pairs), dma(pairs), dma(2, pairs), dma(2), dma(2), dma(2, ys), dma(2, ys), dma(2), dma(2),
        ],
        compiler_params=pltpu.CompilerParams(
            collective_id=0, has_side_effects=True, vmem_limit_bytes=58 * 1024 * 1024),
    )(lengths, accepted, hidden_new.reshape(rounds * batch * R, feats), key_scales, value_scales, queries_draft,
      queries_verify, w_kv, w_out, keys_cache, values_cache,
      key_levels, value_levels)


def solution(mesh):
    return jax.shard_map(
        functools.partial(per_device, mesh.shape["seq"], mesh.shape["tp"]),
        mesh=mesh,
        in_specs=(
            P(None, None, "seq"),
            P("seq", "tp", None),
            P("tp", "seq"),
            P(None, None, "tp", None, None),
            P(None, None, "tp", None, None),
            P(None, "tp", "seq", None),
            P(None, "tp", "seq", None),
            P(None, "tp", "seq", None),
            P(None, "tp", "seq", None),
            P(None, "tp", "seq"),
            P(None, "tp", "seq"),
            P(),
            P(),
        ),
        out_specs=P(None, None, None, "seq"),
        check_vma=False,
    )
```
